128 devices in a mesh: gx: 8 (over z, core), gy: 16 (over x, y).
Axes of the slice: x: 4, y: 4, z: 4, core: 2. Of those that a mesh axis runs over, the one named last changes fastest.
Arguments:
- velocity: float32 [3, 64, 128, 128], P(None, 'gx', 'gy'), may hold values from -1 to 1
- wall_cells: int32 [64, 128, 128], P('gx', 'gy'), may hold values 0 or 1
- tile_counts: int32 [8, 16, 8], P('gx', 'gy'), may hold values from 32 to 256, as said below
- helper_tile: int32 [8, 16], P('gx'), may hold values from 0 to 127, as said below
- base_fields: float32 [8, 16, 8, 3, 32, 1024], P('gx', 'gy'), may hold values from -2.5 to 2.5
- extra_fields: float32 [8, 16, 3, 224, 1024], P('gx', 'gy'), may hold values from -6.1 to 6.1
- base_noise: bfloat16 [8, 16, 8, 2, 3, 32, 1024], P('gx', 'gy'), may hold values from -2.5 to 2.5
- extra_noise: bfloat16 [8, 16, 2, 3, 224, 1024], P('gx', 'gy'), may hold values from -2.5 to 2.5
Outputs:
- new_base_fields: float32 [8, 16, 8, 3, 32, 1024], P('gx', 'gy')
- new_extra_fields: float32 [8, 16, 3, 224, 1024], P('gx', 'gy')
- polymer_stress: float32 [8, 16, 8, 6, 1024], P('gx', 'gy')
The draws below stay inside these ranges and needn't reach their ends.
Inputs may be any that keep to these rules, and one draw needn't show every extreme that they name: `tile_counts`: each entry is 32 or 256. In each row of tiles exactly 16 tiles have 256, these are the tiles that helper_tile names, one column of tiles holds at most 4 of them and in every row some column holds exactly 4. `helper_tile`: entry [i, h] = o * 8 + t names tile t of column o in row i; the entries of a row are distinct and name exactly the row's tiles with 256 fields.
All inputs are finite; a program needn't handle non-finite values. No bound on the sum of `wall_cells` on one device may be relied on, other than what follows from the above.
Results may differ from the reference program's by a relative error of at most 0.0003.
Values sent between devices are 32-bit elements; how exact they have to be, the bound alone decides.
A program may use at most 128 MiB of HBM per device.

```python
import math
import jax
import jax.numpy as jnp

CELL_X = 8
CELL_Y = 8
CELL_Z = 16
T_DEV = 8
BASE_FIELDS = 32
ALL_FIELDS = 256
STEPS = 2
EXTRA_FIELDS = 224
TILE_CELLS = 1024
HEAVY_MOST = 4
TILES_X = 8
TILES_Y = 16
NX = 64
NY = 128
NZ = 128


def heavy_row(row_key, special):
    slot_total = TILES_Y * HEAVY_MOST
    key_score, key_owner, key_tiles, key_helpers = jax.random.split(row_key, 4)
    slot_index = jnp.arange(slot_total, dtype=jnp.int32)
    slot_owner = slot_index // HEAVY_MOST
    slot_local = slot_index % HEAVY_MOST
    scores = jax.random.randint(key_score, (slot_total,), 0, 1048576, dtype=jnp.int32) * slot_total + slot_index
    forced = jax.random.randint(key_owner, (), 0, TILES_Y, dtype=jnp.int32)
    scores = jnp.where(slot_owner == forced, -1 - slot_index, scores)
    edge_slot = (slot_index == 0) | (slot_index == (TILES_Y - 1) * HEAVY_MOST)
    scores = jnp.where(special & edge_slot, -1 - slot_total - slot_index, scores)
    ranking = jnp.argsort(scores)
    chosen = ranking[:TILES_Y]
    tile_scores = jax.random.randint(key_tiles, (TILES_Y, T_DEV), 0, 1048576, dtype=jnp.int32) * T_DEV
    tile_scores = tile_scores + jnp.arange(T_DEV, dtype=jnp.int32)[None, :]
    owner_grid = jnp.arange(TILES_Y, dtype=jnp.int32)[:, None]
    tile_grid = jnp.arange(T_DEV, dtype=jnp.int32)[None, :]
    edge_tile = (owner_grid == 0) & (tile_grid == 0) | (owner_grid == TILES_Y - 1) & (tile_grid == T_DEV - 1)
    tile_scores = jnp.where(special & edge_tile, -1, tile_scores)
    tile_ranking = jnp.argsort(tile_scores, axis=1).astype(jnp.int32)
    chosen_owner = slot_owner[chosen]
    chosen_tile = tile_ranking[chosen_owner, slot_local[chosen]]
    global_ids = chosen_owner * T_DEV + chosen_tile
    helper_order = jax.random.permutation(key_helpers, TILES_Y)
    helper_ids = global_ids[helper_order].astype(jnp.int32)
    heavy_flag = jnp.any(global_ids[:, None] == jnp.arange(TILES_Y * T_DEV, dtype=jnp.int32)[None, :], axis=0)
    counts = jnp.where(heavy_flag, ALL_FIELDS, BASE_FIELDS).astype(jnp.int32).reshape(TILES_Y, T_DEV)
    return (counts, helper_ids)


def heavy_layout(key):
    base_key = jax.random.fold_in(key, 31)
    special_row = jax.random.randint(jax.random.fold_in(key, 77), (), 0, TILES_X, dtype=jnp.int32)
    row_numbers = jnp.arange(TILES_X, dtype=jnp.int32)
    row_keys = jax.vmap(lambda row_number: jax.random.fold_in(base_key, row_number))(row_numbers)
    return jax.vmap(heavy_row)(row_keys, row_numbers == special_row)


def draw_tile_counts(key, part):
    return heavy_layout(key)[0]


def draw_helper_tile(key, part):
    return heavy_layout(key)[1]


def draw_base_fields(key, part):
    key_scale, key_values = jax.random.split(jax.random.fold_in(key, 101))
    low_scale, high_scale = (0.5, 2.0)
    log_scale = jax.random.uniform(key_scale, (TILES_X, TILES_Y, T_DEV, 1, 1, TILE_CELLS), jnp.float32, math.log(low_scale), math.log(high_scale))
    values = jax.random.uniform(key_values, (TILES_X, TILES_Y, T_DEV, 3, BASE_FIELDS, TILE_CELLS), jnp.float32, -1.0, 1.0)
    return jnp.exp(log_scale) * values


def draw_extra_fields(key, part):
    key_stretch, key_radius, key_direction = jax.random.split(jax.random.fold_in(key, 202), 3)
    low_square, low_radius = (12.0, 0.8)
    log_square = jax.random.uniform(key_stretch, (TILES_X, TILES_Y, 1, 1, TILE_CELLS), jnp.float32, math.log(low_square), math.log(30.0))
    radius = jax.random.uniform(key_radius, (TILES_X, TILES_Y, 1, EXTRA_FIELDS, TILE_CELLS), jnp.float32, low_radius, 1.1)
    direction = jax.random.normal(key_direction, (TILES_X, TILES_Y, 3, EXTRA_FIELDS, TILE_CELLS), jnp.float32)
    length = jnp.sqrt(jnp.sum(direction * direction, axis=2, keepdims=True) + 1e-12)
    return jnp.exp(0.5 * log_square) * radius * (direction / length)


def plant(entries, own_key, smallest, high):
    longest = entries.shape.index(max(entries.shape))
    spots = []
    for shift in (0, 1):
        where = [jax.random.randint(jax.random.fold_in(own_key, axis), (), 0, length) for axis, length in enumerate(entries.shape)]
        where[longest] = (where[longest] + shift) % entries.shape[longest]
        spots.append(tuple(where))
    return entries.at[spots[0]].set(smallest).at[spots[1]].set(high)


def level_of(own_key, extent, cuts, smallest, high):
    gain, own = 1.0, jax.random.fold_in(own_key, 6)
    for axis_at, shards_of in cuts:
        steps = jnp.exp(jax.random.uniform(jax.random.fold_in(own, axis_at), (shards_of,), jnp.float32, smallest / len(cuts), high / len(cuts)))
        gain = gain * jnp.repeat(steps, extent[axis_at] // shards_of).reshape([-1 if axis == axis_at else 1 for axis in range(len(extent))])
    return gain


def scatter_about(stream_key, extent, spread, reach, shards=(), held_as=jnp.bfloat16):
    result = spread * jax.random.normal(stream_key, extent, jnp.float32)
    if shards:
        result = result * level_of(stream_key, extent, shards, -0.22, 0.18)
    return jnp.clip(result, -reach, reach).astype(held_as)


def setup_inputs(seed: int = 0) -> dict:
    arg_keys = jax.random.split(jax.random.key(seed), 9)
    velocity = jnp.clip(jax.random.uniform(arg_keys[0], (3, NX, NY, NZ), jnp.float32, -1.0, 1.0) * level_of(arg_keys[0], (3, NX, NY, NZ), ((1, 8), (2, 16)), -0.4, 0.0), -1.0, 1.0)
    wall_cells = plant((jax.random.randint(arg_keys[1], (NX, NY, NZ), 0, 8) < 1).astype(jnp.int32), jax.random.fold_in(arg_keys[1], 1), 0, 1)
    tile_counts = draw_tile_counts(jax.random.fold_in(arg_keys[8], 71), 0)
    helper_tile = draw_helper_tile(jax.random.fold_in(arg_keys[8], 71), 0)
    base_fields = draw_base_fields(jax.random.fold_in(arg_keys[8], 71), 0)
    extra_fields = draw_extra_fields(jax.random.fold_in(arg_keys[8], 71), 0)
    base_noise = scatter_about(arg_keys[6], (TILES_X, TILES_Y, T_DEV, STEPS, 3, BASE_FIELDS, TILE_CELLS), 1.0, 2.5, ((0, 8), (1, 16)))
    extra_noise = scatter_about(arg_keys[7], (TILES_X, TILES_Y, STEPS, 3, EXTRA_FIELDS, TILE_CELLS), 1.0, 2.5, ((0, 8), (1, 16)))
    return {"velocity": velocity, "wall_cells": wall_cells, "tile_counts": tile_counts, "helper_tile": helper_tile, "base_fields": base_fields, "extra_fields": extra_fields, "base_noise": base_noise, "extra_noise": extra_noise}


time_step = 0.05
weissenberg = 0.25
max_extension = 50.0
noise_scale = (time_step / weissenberg) ** 0.5
component_pairs = ((0, 0), (1, 1), (2, 2), (0, 1), (0, 2), (1, 2))


def velocity_gradient(padded, wall_cells):
    along_x = (padded[:, 2:, 1:-1, 1:-1] - padded[:, :-2, 1:-1, 1:-1]) * 0.5
    along_y = (padded[:, 1:-1, 2:, 1:-1] - padded[:, 1:-1, :-2, 1:-1]) * 0.5
    along_z = (padded[:, 1:-1, 1:-1, 2:] - padded[:, 1:-1, 1:-1, :-2]) * 0.5
    fluid = (wall_cells == 0).astype(jnp.float32)
    stacked = jnp.stack([along_x, along_y, along_z], axis=1) * fluid
    return stacked.reshape((9,) + wall_cells.shape)


def spring_factor(total, count):
    return 1.0 / (1.0 - (total / count) / max_extension)


def advance(state, grad, factor, noise):
    relax = factor[..., None, :] * (0.5 / weissenberg)
    parts = []
    for component in range(3):
        drift = grad[..., 3 * component, None, :] * state[..., 0, :, :]
        drift = drift + grad[..., 3 * component + 1, None, :] * state[..., 1, :, :]
        drift = drift + grad[..., 3 * component + 2, None, :] * state[..., 2, :, :]
        current = state[..., component, :, :]
        parts.append(current + time_step * (drift - relax * current)
                     + noise_scale * noise[..., component, :, :].astype(jnp.float32))
    return jnp.stack(parts, axis=-3)


def moments(state):
    return jnp.stack([jnp.sum(state[..., first_axis, :, :] * state[..., second_axis, :, :], axis=-2)
                      for first_axis, second_axis in component_pairs], axis=-2)


def polymer_stress(total, count):
    second = total / count
    trace = second[..., 0, :] + second[..., 1, :] + second[..., 2, :]
    stretch = 1.0 / (1.0 - trace / max_extension)
    unit = jnp.array([1.0, 1.0, 1.0, 0.0, 0.0, 0.0], jnp.float32)[:, None]
    return (stretch[..., None, :] * second - unit) / weissenberg


def add_helpers(own_rows, extra_rows, helper_tile):
    row_index = jnp.arange(TILES_X, dtype=jnp.int32)[:, None]
    flat = own_rows.reshape((TILES_X, TILES_Y * T_DEV) + own_rows.shape[3:])
    flat = flat.at[row_index, helper_tile].add(extra_rows)
    return flat.reshape(own_rows.shape)


def reference(velocity, wall_cells, tile_counts, helper_tile, base_fields, extra_fields, base_noise, extra_noise):
    padded = jnp.pad(velocity, ((0, 0), (1, 1), (1, 1), (1, 1)))
    grad_grid = velocity_gradient(padded, wall_cells)
    tile_grad = grad_grid.reshape(9, TILES_X, CELL_X, TILES_Y, CELL_Y, T_DEV, CELL_Z)
    tile_grad = tile_grad.transpose(1, 3, 5, 0, 2, 4, 6).reshape(TILES_X, TILES_Y, T_DEV, 9, TILE_CELLS)
    row_index = jnp.arange(TILES_X, dtype=jnp.int32)[:, None]
    helper_grad = tile_grad.reshape(TILES_X, TILES_Y * T_DEV, 9, TILE_CELLS)[row_index, helper_tile]
    counts = tile_counts.astype(jnp.float32)
    base_state = base_fields
    extra_state = extra_fields
    for step_index in range(STEPS):
        base_square = jnp.sum(base_state * base_state, axis=(3, 4))
        extra_square = jnp.sum(extra_state * extra_state, axis=(2, 3))
        tile_total = add_helpers(base_square, extra_square, helper_tile)
        factor = spring_factor(tile_total, counts[..., None])
        helper_factor = factor.reshape(TILES_X, TILES_Y * T_DEV, TILE_CELLS)[row_index, helper_tile]
        base_state = advance(base_state, tile_grad, factor, base_noise[:, :, :, step_index])
        extra_state = advance(extra_state, helper_grad, helper_factor, extra_noise[:, :, step_index])
    moment_total = add_helpers(moments(base_state), moments(extra_state), helper_tile)
    stress = polymer_stress(moment_total, counts[..., None, None])
    return base_state, extra_state, stress
```

```python
import functools

import jax
import jax.numpy as jnp
from jax import lax
from jax.experimental import pallas as pl
from jax.experimental.pallas import tpu as pltpu
from jax.sharding import PartitionSpec as P

MESH = pl.DeviceIdType.MESH
F32 = jnp.float32

STEPS = 2
TILES = 8
CELLS = 1024
LANES = 128
CHUNKS = CELLS // LANES
BASE = 32
EXTRA = 224
GROUP = 32

time_step = 0.05
weissenberg = 0.25
max_extension = 50.0
noise_scale = (time_step / weissenberg) ** 0.5
relax_scale = time_step * (0.5 / weissenberg)
component_pairs = ((0, 0), (1, 1), (2, 2), (0, 1), (0, 2), (1, 2))


def wide(row):
    return jnp.broadcast_to(row, (GROUP, LANES))


def matrix(grad_row, relax_row):
    keep = wide(1.0 - relax_row)
    rows = []
    for a in range(3):
        row = [wide(grad_row(3 * a + b)) for b in range(3)]
        row[a] = row[a] + keep
        rows.append(row)
    return rows


def advance(mat, state, noise):
    return [
        mat[a][0] * state[0]
        + mat[a][1] * state[1]
        + mat[a][2] * state[2]
        + noise_scale * noise[a].astype(F32)
        for a in range(3)
    ]


def fold(block):
    out = block[:8]
    for k in range(1, block.shape[0] // 8):
        out = out + block[8 * k : 8 * k + 8]
    return out


def squares(state):
    return fold(state[0] * state[0] + state[1] * state[1] + state[2] * state[2])


def products(state):
    return [fold(state[a] * state[b]) for a, b in component_pairs]


def row_sum(block):
    return jnp.sum(block, axis=0, keepdims=True)


def kernel(
    n_gx,
    n_gy,
    counts,
    helper,
    vel_hbm,
    wall_hbm,
    base_hbm,
    extra_hbm,
    base_noise_hbm,
    extra_noise_hbm,
    base,
    extra,
    stress,
    vel,
    wall,
    base_noise,
    extra_noise,
    y_edge,
    x_halo,
    y_halo,
    tile_grad,
    helper_grad,
    grad_send,
    grad_recv,
    own_sum,
    extra_sum,
    sum_send,
    first_recv,
    second_recv,
    relax,
    helper_relax,
    own_moment,
    moment_recv,
    in_sem,
    tile_sem,
    halo_send_sem,
    halo_recv_sem,
    grad_send_sem,
    grad_recv_sem,
    sum_send_sem,
    sum_recv_sem,
    moment_send_sem,
    moment_recv_sem,
):
    gx = lax.axis_index("gx")
    gy = lax.axis_index("gy")
    up_x, down_x = lax.rem(gx + 1, n_gx), lax.rem(gx + n_gx - 1, n_gx)
    up_y, down_y = lax.rem(gy + 1, n_gy), lax.rem(gy + n_gy - 1, n_gy)

    vel_copy = pltpu.make_async_copy(vel_hbm, vel, in_sem.at[0])
    wall_copy = pltpu.make_async_copy(wall_hbm, wall, in_sem.at[1])
    extra_copy = pltpu.make_async_copy(extra_hbm, extra, in_sem.at[2])
    base_copies = [
        pltpu.make_async_copy(base_hbm.at[t], base.at[t], tile_sem.at[t]) for t in range(TILES)
    ]
    base_noise_copies = [
        pltpu.make_async_copy(base_noise_hbm.at[:, s], base_noise.at[s], in_sem.at[3 + s])
        for s in range(STEPS)
    ]
    extra_noise_copies = [
        pltpu.make_async_copy(extra_noise_hbm.at[s], extra_noise.at[s], in_sem.at[5 + s])
        for s in range(STEPS)
    ]
    vel_copy.start()
    wall_copy.start()
    for copy in base_copies:
        copy.start()
    extra_copy.start()
    for s in range(STEPS):
        base_noise_copies[s].start()
        extra_noise_copies[s].start()

    barrier = pltpu.get_barrier_semaphore()
    for k in range(1, n_gy):
        peer = lax.rem(gy + k, n_gy)
        pl.semaphore_signal(barrier, inc=1, device_id=(gx, peer), device_id_type=MESH)
    for peer in (up_x, down_x):
        pl.semaphore_signal(barrier, inc=1, device_id=(peer, gy), device_id_type=MESH)

    my_tile = helper[gy]
    my_slot = lax.rem(gy - my_tile // TILES + n_gy, n_gy)
    slot_of, found = [], []
    for t in range(TILES):
        slot, hit = jnp.int32(0), jnp.int32(0)
        for h in range(n_gy):
            match = helper[h] == gy * TILES + t
            slot = jnp.where(match, lax.rem(gy - h + n_gy, n_gy), slot)
            hit = jnp.where(match, 1, hit)
        slot_of.append(slot)
        found.append(hit)

    vel_copy.wait()
    for c in range(3):
        y_edge[0, c] = vel[c, :, 7, :]
        y_edge[1, c] = vel[c, :, 0, :]
    pl.semaphore_wait(barrier, n_gy + 1)

    halo_copies = [
        pltpu.make_async_remote_copy(
            src_ref=src,
            dst_ref=dst,
            send_sem=halo_send_sem.at[i],
            recv_sem=halo_recv_sem.at[i],
            device_id=device,
            device_id_type=MESH,
        )
        for i, (src, dst, device) in enumerate(
            (
                (vel.at[:, 7], x_halo.at[0], (up_x, gy)),
                (vel.at[:, 0], x_halo.at[1], (down_x, gy)),
                (y_edge.at[0], y_halo.at[0], (gx, up_y)),
                (y_edge.at[1], y_halo.at[1], (gx, down_y)),
            )
        )
    ]
    for copy in halo_copies:
        copy.start()

    def peer_copies(src_of, dst_of, send_sem, recv_sem):
        return [
            pltpu.make_async_remote_copy(
                src_ref=src_of(k),
                dst_ref=dst_of(k),
                send_sem=send_sem(k),
                recv_sem=recv_sem(k),
                device_id=(gx, lax.rem(gy + k, n_gy)),
                device_id_type=MESH,
            )
            for k in range(1, n_gy)
        ]

    sum_recv = (first_recv, second_recv)

    def sum_exchange(r):
        @pl.loop(0, n_gy)
        def _(k):
            tile = lax.rem(helper[lax.rem(gy + k, n_gy)], TILES)
            sum_send[r, k, 0] = own_sum[tile]
            sum_send[r, k, 1] = extra_sum[...]

        copies = peer_copies(
            lambda k: sum_send.at[r, k],
            lambda k: sum_recv[r].at[k],
            lambda k: sum_send_sem.at[r, k],
            lambda k: sum_recv_sem.at[r, k],
        )
        for copy in copies:
            copy.start()
        sum_recv[r][0] = sum_send[r, 0]
        return copies

    def factors(r, copies):
        for copy in copies:
            copy.wait_recv()
        for t in range(TILES):
            count = jnp.full((CHUNKS, LANES), counts[t], jnp.int32).astype(F32)
            total = own_sum[t] + jnp.where(found[t] == 1, sum_recv[r][slot_of[t], 1], 0.0)
            relax[t] = relax_scale * (1.0 / (1.0 - total / count / max_extension))
        total = extra_sum[...] + sum_recv[r][my_slot, 0]
        helper_relax[...] = relax_scale * (1.0 / (1.0 - total / 256.0 / max_extension))

    for copy in base_copies:
        copy.wait()

    @pl.loop(0, TILES)
    def _(t):
        for x in range(CHUNKS):
            lanes = pl.ds(x * LANES, LANES)
            state = [base[t, c, :, lanes] for c in range(3)]
            own_sum[t, pl.ds(x, 1), :] = row_sum(squares(state))

    extra_copy.wait()

    @pl.loop(0, CHUNKS)
    def _(x):
        lanes = pl.ds(pl.multiple_of(x * LANES, LANES), LANES)
        total = jnp.zeros((8, LANES), F32)
        for f in range(EXTRA // GROUP):
            fields = pl.ds(f * GROUP, GROUP)
            total = total + squares([extra[c, fields, lanes] for c in range(3)])
        extra_sum[pl.ds(x, 1), :] = row_sum(total)

    first_sums = sum_exchange(0)

    wall_copy.wait()
    for copy in halo_copies:
        copy.wait_recv()
    sub = lax.broadcasted_iota(jnp.int32, (8, LANES), 0)
    lane = lax.broadcasted_iota(jnp.int32, (8, LANES), 1)
    block = lane // 16
    fluid = [
        jnp.where(wall[:, y, :] == 0, 0.5 * time_step, 0.0).astype(F32) for y in range(8)
    ]
    for a in range(3):
        here = [vel[a, :, y, :] for y in range(8)]
        low_y = jnp.where(gy > 0, y_halo[0, a], 0.0)
        high_y = jnp.where(gy < n_gy - 1, y_halo[1, a], 0.0)
        padded = [low_y] + here + [high_y]
        low_x = jnp.where(gx > 0, x_halo[0, a], 0.0)
        high_x = jnp.where(gx < n_gx - 1, x_halo[1, a], 0.0)
        columns = [[], [], []]
        for y in range(8):
            v = here[y]
            low = jnp.broadcast_to(low_x[y : y + 1], (8, LANES))
            high = jnp.broadcast_to(high_x[y : y + 1], (8, LANES))
            before = jnp.where(sub == 0, low, pltpu.roll(v, 1, 0))
            after = jnp.where(sub == 7, high, pltpu.roll(v, 7, 0))
            columns[0].append((after - before) * fluid[y])
            columns[1].append((padded[y + 2] - padded[y]) * fluid[y])
            before = jnp.where(lane == 0, 0.0, pltpu.roll(v, 1, 1))
            after = jnp.where(lane == LANES - 1, 0.0, pltpu.roll(v, LANES - 1, 1))
            columns[2].append((after - before) * fluid[y])
        for b in range(3):
            regs = columns[b]
            for bit in (1, 2, 4):
                upper = (block & bit) != 0
                new = list(regs)
                for i in range(8):
                    if i & bit:
                        continue
                    j = i | bit
                    new[i] = jnp.where(upper, pltpu.roll(regs[j], 16 * bit, 1), regs[i])
                    new[j] = jnp.where(upper, regs[j], pltpu.roll(regs[i], LANES - 16 * bit, 1))
                regs = new
            for t in range(TILES):
                tile_grad[t, 3 * a + b] = regs[t]

    @pl.loop(0, n_gy)
    def _(k):
        tile = lax.rem(helper[lax.rem(gy + k, n_gy)], TILES)
        grad_send[k] = tile_grad[tile]

    grad_copies = peer_copies(
        lambda k: grad_send.at[k],
        lambda k: grad_recv.at[k],
        lambda k: grad_send_sem.at[k],
        lambda k: grad_recv_sem.at[k],
    )
    for copy in grad_copies:
        copy.start()
    grad_recv[0] = grad_send[0]

    factors(0, first_sums)

    base_noise_copies[0].wait()

    @pl.loop(0, TILES)
    def _(t):
        for x in range(CHUNKS):
            lanes = pl.ds(x * LANES, LANES)
            mat = matrix(lambda c: tile_grad[t, c, pl.ds(x, 1), :], relax[t, pl.ds(x, 1), :])
            state = [base[t, c, :, lanes] for c in range(3)]
            noise = [base_noise[0, t, c, :, lanes] for c in range(3)]
            state = advance(mat, state, noise)
            for c in range(3):
                base[t, c, :, lanes] = state[c]
            own_sum[t, pl.ds(x, 1), :] = row_sum(squares(state))

    for copy in grad_copies:
        copy.wait_recv()
    helper_grad[...] = grad_recv[my_slot]
    extra_noise_copies[0].wait()

    @pl.loop(0, CHUNKS)
    def _(x):
        lanes = pl.ds(pl.multiple_of(x * LANES, LANES), LANES)
        mat = matrix(lambda c: helper_grad[c, pl.ds(x, 1), :], helper_relax[pl.ds(x, 1), :])
        total = jnp.zeros((8, LANES), F32)
        for f in range(EXTRA // GROUP):
            fields = pl.ds(f * GROUP, GROUP)
            state = [extra[c, fields, lanes] for c in range(3)]
            noise = [extra_noise[0, c, fields, lanes] for c in range(3)]
            state = advance(mat, state, noise)
            for c in range(3):
                extra[c, fields, lanes] = state[c]
            total = total + squares(state)
        extra_sum[pl.ds(x, 1), :] = row_sum(total)

    second_sums = sum_exchange(1)
    extra_noise_copies[1].wait()
    base_noise_copies[1].wait()
    factors(1, second_sums)

    @pl.loop(0, CHUNKS)
    def _(x):
        lanes = pl.ds(pl.multiple_of(x * LANES, LANES), LANES)
        mat = matrix(lambda c: helper_grad[c, pl.ds(x, 1), :], helper_relax[pl.ds(x, 1), :])
        totals = [jnp.zeros((8, LANES), F32) for _ in range(6)]
        for f in range(EXTRA // GROUP):
            fields = pl.ds(f * GROUP, GROUP)
            state = [extra[c, fields, lanes] for c in range(3)]
            noise = [extra_noise[1, c, fields, lanes] for c in range(3)]
            state = advance(mat, state, noise)
            for c in range(3):
                extra[c, fields, lanes] = state[c]
            totals = [u + v for u, v in zip(totals, products(state))]
        for m in range(6):
            moment_recv[0, m, pl.ds(x, 1), :] = row_sum(totals[m])

    moment_copies = peer_copies(
        lambda k: moment_recv.at[0],
        lambda k: moment_recv.at[k],
        lambda k: moment_send_sem.at[k],
        lambda k: moment_recv_sem.at[k],
    )
    for copy in moment_copies:
        copy.start()

    @pl.loop(0, TILES)
    def _(t):
        for x in range(CHUNKS):
            lanes = pl.ds(x * LANES, LANES)
            mat = matrix(lambda c: tile_grad[t, c, pl.ds(x, 1), :], relax[t, pl.ds(x, 1), :])
            state = [base[t, c, :, lanes] for c in range(3)]
            noise = [base_noise[1, t, c, :, lanes] for c in range(3)]
            state = advance(mat, state, noise)
            for c in range(3):
                base[t, c, :, lanes] = state[c]
            for m, total in enumerate(products(state)):
                own_moment[t, m, pl.ds(x, 1), :] = row_sum(total)

    for copy in moment_copies:
        copy.wait_recv()
    for t in range(TILES):
        count = jnp.full((CHUNKS, LANES), counts[t], jnp.int32).astype(F32)
        second = [
            (own_moment[t, m] + jnp.where(found[t] == 1, moment_recv[slot_of[t], m], 0.0)) / count
            for m in range(6)
        ]
        trace = second[0] + second[1] + second[2]
        stretch = 1.0 / (1.0 - trace / max_extension)
        for m in range(6):
            value = (stretch * second[m] - (1.0 if m < 3 else 0.0)) / weissenberg
            for x in range(CHUNKS):
                stress[m, pl.ds(t, 1), pl.ds(x * LANES, LANES)] = value[x : x + 1]

    for copies in (halo_copies, first_sums, grad_copies, second_sums, moment_copies):
        for copy in copies:
            copy.wait_send()


def solution(mesh):
    n_gx, n_gy = mesh.shape["gx"], mesh.shape["gy"]

    def per_device(
        velocity,
        wall_cells,
        tile_counts,
        helper_tile,
        base_fields,
        extra_fields,
        base_noise,
        extra_noise,
    ):
        hbm_spec = pl.BlockSpec(memory_space=pltpu.HBM)
        vmem_spec = pl.BlockSpec(memory_space=pltpu.VMEM)
        smem_spec = pl.BlockSpec(memory_space=pltpu.SMEM)
        dma = pltpu.SemaphoreType.DMA

        def hold(array):
            return pltpu.with_memory_space_constraint(array, pltpu.HBM)

        base_out, extra_out, stress_out = pl.pallas_call(
            functools.partial(kernel, n_gx, n_gy),
            out_shape=(
                jax.ShapeDtypeStruct((TILES, 3, BASE, CELLS), F32),
                jax.ShapeDtypeStruct((3, EXTRA, CELLS), F32),
                jax.ShapeDtypeStruct((6, TILES, CELLS), F32),
            ),
            in_specs=[smem_spec, smem_spec] + [hbm_spec] * 6,
            out_specs=(vmem_spec, vmem_spec, vmem_spec),
            scratch_shapes=[
                pltpu.VMEM((3, 8, 8, LANES), F32),
                pltpu.VMEM((8, 8, LANES), jnp.int32),
                pltpu.VMEM((STEPS, TILES, 3, BASE, CELLS), jnp.bfloat16),
                pltpu.VMEM((STEPS, 3, EXTRA, CELLS), jnp.bfloat16),
                pltpu.VMEM((2, 3, 8, LANES), F32),
                pltpu.VMEM((2, 3, 8, LANES), F32),
                pltpu.VMEM((2, 3, 8, LANES), F32),
                pltpu.VMEM((TILES, 9, CHUNKS, LANES), F32),
                pltpu.VMEM((9, CHUNKS, LANES), F32),
                pltpu.VMEM((n_gy, 9, CHUNKS, LANES), F32),
                pltpu.VMEM((n_gy, 9, CHUNKS, LANES), F32),
                pltpu.VMEM((TILES, CHUNKS, LANES), F32),
                pltpu.VMEM((CHUNKS, LANES), F32),
                pltpu.VMEM((STEPS, n_gy, 2, CHUNKS, LANES), F32),
                pltpu.VMEM((n_gy, 2, CHUNKS, LANES), F32),
                pltpu.VMEM((n_gy, 2, CHUNKS, LANES), F32),
                pltpu.VMEM((TILES, CHUNKS, LANES), F32),
                pltpu.VMEM((CHUNKS, LANES), F32),
                pltpu.VMEM((TILES, 6, CHUNKS, LANES), F32),
                pltpu.VMEM((n_gy, 6, CHUNKS, LANES), F32),
                dma((7,)),
                dma((TILES,)),
                dma((4,)),
                dma((4,)),
                dma((n_gy,)),
                dma((n_gy,)),
                dma((STEPS, n_gy)),
                dma((STEPS, n_gy)),
                dma((n_gy,)),
                dma((n_gy,)),
            ],
            compiler_params=pltpu.CompilerParams(
                collective_id=0, has_side_effects=True, vmem_limit_bytes=40 << 20
            ),
        )(
            hold(tile_counts.reshape(TILES)),
            hold(helper_tile.reshape(n_gy)),
            hold(velocity),
            hold(wall_cells),
            hold(base_fields.reshape(TILES, 3, BASE, CELLS)),
            hold(extra_fields.reshape(3, EXTRA, CELLS)),
            hold(base_noise.reshape(TILES, STEPS, 3, BASE, CELLS)),
            hold(extra_noise.reshape(STEPS, 3, EXTRA, CELLS)),
        )
        return base_out[None, None], extra_out[None, None], stress_out.transpose(1, 0, 2)[None, None]

    in_specs = (
        P(None, "gx", "gy", None),
        P("gx", "gy", None),
        P("gx", "gy", None),
        P("gx", None),
        P("gx", "gy", None, None, None, None),
        P("gx", "gy", None, None, None),
        P("gx", "gy", None, None, None, None, None),
        P("gx", "gy", None, None, None, None),
    )
    out_specs = (
        P("gx", "gy", None, None, None, None),
        P("gx", "gy", None, None, None),
        P("gx", "gy", None, None, None),
    )
    return jax.shard_map(
        per_device, mesh=mesh, in_specs=in_specs, out_specs=out_specs, check_vma=False
    )
```

```python
import functools

import jax
import jax.numpy as jnp
from jax import lax
from jax.experimental import pallas as pl
from jax.experimental.pallas import tpu as pltpu
from jax.sharding import PartitionSpec as P

MESH = pl.DeviceIdType.MESH
F32 = jnp.float32

STEPS = 2
TILES = 8
CELLS = 1024
LANES = 128
CHUNKS = CELLS // LANES
BASE = 32
EXTRA = 224
GROUP = 32
PARTS = 2
ROWS = CHUNKS // PARTS

time_step = 0.05
weissenberg = 0.25
max_extension = 50.0
noise_scale = (time_step / weissenberg) ** 0.5
relax_scale = time_step * (0.5 / weissenberg)
component_pairs = ((0, 0), (1, 1), (2, 2), (0, 1), (0, 2), (1, 2))


def wide(row):
    return jnp.broadcast_to(row, (GROUP, LANES))


def matrix(grad_row, keep_row):
    keep = wide(keep_row)
    rows = []
    for a in range(3):
        row = [wide(grad_row(3 * a + b)) for b in range(3)]
        row[a] = row[a] + keep
        rows.append(row)
    return rows


def advance(mat, state, noise):
    return [
        mat[a][0] * state[0]
        + mat[a][1] * state[1]
        + mat[a][2] * state[2]
        + noise_scale * noise[a].astype(F32)
        for a in range(3)
    ]


def fold(block):
    out = block[:8]
    for k in range(1, block.shape[0] // 8):
        out = out + block[8 * k : 8 * k + 8]
    return out


def inner(left, right):
    return fold(left[0] * right[0] + left[1] * right[1] + left[2] * right[2])


def products(state):
    return [fold(state[a] * state[b]) for a, b in component_pairs]


def row_sum(block):
    return jnp.sum(block, axis=0, keepdims=True)


def relaxation(total, count):
    return relax_scale * (1.0 / (1.0 - total / count / max_extension))


def part_of(value, p):
    return value[p * ROWS : (p + 1) * ROWS]


def helper_slots(helper, gy, n_gy, t):
    slot, hit = jnp.int32(0), jnp.int32(0)
    for h in range(n_gy):
        match = helper[h] == gy * TILES + t
        slot = jnp.where(match, lax.rem(gy - h + n_gy, n_gy), slot)
        hit = jnp.where(match, 1, hit)
    return slot, hit


def exchange_kernel(
    n_gx,
    n_gy,
    counts,
    helper,
    vel_hbm,
    wall_hbm,
    base_hbm,
    extra_hbm,
    base_noise_hbm,
    extra_noise_hbm,
    base,
    extra,
    late_noise,
    tile_grad,
    own_total,
    moment_recv,
    vel,
    wall,
    drifted,
    base_noise,
    extra_noise,
    y_edge,
    x_halo,
    y_halo,
    own_sums,
    extra_sum,
    extra_recv,
    own_send,
    own_recv,
    helper_relax,
    helper_total,
    row_total,
    relax,
    *rest,
):
    grad_send, grad_recv = rest[:PARTS], rest[PARTS : 2 * PARTS]
    (
        in_sem,
        tile_sem,
        halo_send_sem,
        halo_recv_sem,
        extra_send_sem,
        extra_recv_sem,
        own_send_sem,
        own_recv_sem,
        grad_send_sem,
        grad_recv_sem,
        moment_send_sem,
        moment_recv_sem,
    ) = rest[2 * PARTS :]
    gx = lax.axis_index("gx")
    gy = lax.axis_index("gy")
    up_x, down_x = lax.rem(gx + 1, n_gx), lax.rem(gx + n_gx - 1, n_gx)
    up_y, down_y = lax.rem(gy + 1, n_gy), lax.rem(gy + n_gy - 1, n_gy)

    vel_copy = pltpu.make_async_copy(vel_hbm, vel, in_sem.at[0])
    wall_copy = pltpu.make_async_copy(wall_hbm, wall, in_sem.at[1])
    extra_copy = pltpu.make_async_copy(extra_hbm, extra, in_sem.at[2])
    base_copies = [
        pltpu.make_async_copy(base_hbm.at[t], base.at[t], tile_sem.at[t]) for t in range(TILES)
    ]
    base_noise_copies = [
        pltpu.make_async_copy(base_noise_hbm.at[:, 0], base_noise, in_sem.at[3]),
        pltpu.make_async_copy(base_noise_hbm.at[:, 1], late_noise, in_sem.at[4]),
    ]
    extra_noise_copies = [
        pltpu.make_async_copy(extra_noise_hbm.at[s], extra_noise.at[s], in_sem.at[5 + s])
        for s in range(STEPS)
    ]
    vel_copy.start()
    wall_copy.start()
    extra_copy.start()
    for copy in base_copies:
        copy.start()
    for s in range(STEPS):
        base_noise_copies[s].start()
        extra_noise_copies[s].start()

    barrier = pltpu.get_barrier_semaphore()
    for k in range(1, n_gy):
        peer = lax.rem(gy + k, n_gy)
        pl.semaphore_signal(barrier, inc=1, device_id=(gx, peer), device_id_type=MESH)
    for peer in (up_x, down_x):
        pl.semaphore_signal(barrier, inc=1, device_id=(peer, gy), device_id_type=MESH)

    my_slot = lax.rem(gy - helper[gy] // TILES + n_gy, n_gy)
    slots = [helper_slots(helper, gy, n_gy, t) for t in range(TILES)]

    vel_copy.wait()
    for c in range(3):
        y_edge[0, c] = vel[c, :, 7, :]
        y_edge[1, c] = vel[c, :, 0, :]
    pl.semaphore_wait(barrier, n_gy + 1)

    halo_copies = [
        pltpu.make_async_remote_copy(
            src_ref=src,
            dst_ref=dst,
            send_sem=halo_send_sem.at[i],
            recv_sem=halo_recv_sem.at[i],
            device_id=device,
            device_id_type=MESH,
        )
        for i, (src, dst, device) in enumerate(
            (
                (vel.at[:, 7], x_halo.at[0], (up_x, gy)),
                (vel.at[:, 0], x_halo.at[1], (down_x, gy)),
                (y_edge.at[0], y_halo.at[0], (gx, up_y)),
                (y_edge.at[1], y_halo.at[1], (gx, down_y)),
            )
        )
    ]
    for copy in halo_copies:
        copy.start()

    def send_all(src_of, dst_of, send_sem, recv_sem):
        copies = [
            pltpu.make_async_remote_copy(
                src_ref=src_of(k),
                dst_ref=dst_of(k),
                send_sem=send_sem(k),
                recv_sem=recv_sem(k),
                device_id=(gx, lax.rem(gy + k, n_gy)),
                device_id_type=MESH,
            )
            for k in range(1, n_gy)
        ]
        for copy in copies:
            copy.start()
        return copies

    extra_copy.wait()

    @pl.loop(0, CHUNKS)
    def _(x):
        lanes = pl.ds(pl.multiple_of(x * LANES, LANES), LANES)
        total = jnp.zeros((8, LANES), F32)
        for f in range(EXTRA // GROUP):
            state = [extra[c, pl.ds(f * GROUP, GROUP), lanes] for c in range(3)]
            total = total + inner(state, state)
        extra_sum[pl.ds(x, 1), :] = row_sum(total)

    wall_copy.wait()
    for copy in halo_copies:
        copy.wait_recv()
    sub = lax.broadcasted_iota(jnp.int32, (8, LANES), 0)
    lane = lax.broadcasted_iota(jnp.int32, (8, LANES), 1)
    block = lane // 16
    fluid = [
        jnp.where(wall[:, y, :] == 0, 0.5 * time_step, 0.0).astype(F32) for y in range(8)
    ]
    for a in range(3):
        here = [vel[a, :, y, :] for y in range(8)]
        low_y = jnp.where(gy > 0, y_halo[0, a], 0.0)
        high_y = jnp.where(gy < n_gy - 1, y_halo[1, a], 0.0)
        padded = [low_y] + here + [high_y]
        low_x = jnp.where(gx > 0, x_halo[0, a], 0.0)
        high_x = jnp.where(gx < n_gx - 1, x_halo[1, a], 0.0)
        columns = [[], [], []]
        for y in range(8):
            v = here[y]
            low = jnp.broadcast_to(low_x[y : y + 1], (8, LANES))
            high = jnp.broadcast_to(high_x[y : y + 1], (8, LANES))
            before = jnp.where(sub == 0, low, pltpu.roll(v, 1, 0))
            after = jnp.where(sub == 7, high, pltpu.roll(v, 7, 0))
            columns[0].append((after - before) * fluid[y])
            columns[1].append((padded[y + 2] - padded[y]) * fluid[y])
            before = jnp.where(lane == 0, 0.0, pltpu.roll(v, 1, 1))
            after = jnp.where(lane == LANES - 1, 0.0, pltpu.roll(v, LANES - 1, 1))
            columns[2].append((after - before) * fluid[y])
        for b in range(3):
            regs = columns[b]
            for bit in (1, 2, 4):
                upper = (block & bit) != 0
                new = list(regs)
                for i in range(8):
                    if i & bit:
                        continue
                    j = i | bit
                    new[i] = jnp.where(upper, pltpu.roll(regs[j], 16 * bit, 1), regs[i])
                    new[j] = jnp.where(upper, regs[j], pltpu.roll(regs[i], LANES - 16 * bit, 1))
                regs = new
            for t in range(TILES):
                for p in range(PARTS):
                    tile_grad[t, p, 3 * a + b] = part_of(regs[t], p)

    extra_copies = send_all(
        lambda k: extra_sum,
        lambda k: extra_recv.at[k],
        lambda k: extra_send_sem.at[k],
        lambda k: extra_recv_sem.at[k],
    )
    extra_recv[0] = extra_sum[...]

    grad_copies = []
    for p in range(PARTS):

        @pl.loop(0, n_gy)
        def _(k):
            tile = lax.rem(helper[lax.rem(gy + k, n_gy)], TILES)
            grad_send[p][k] = tile_grad[tile, p]

        grad_copies.append(
            send_all(
                lambda k: grad_send[p].at[k],
                lambda k: grad_recv[p].at[k],
                lambda k: grad_send_sem.at[p, k],
                lambda k: grad_recv_sem.at[p, k],
            )
        )
        grad_recv[p][0] = grad_send[p][0]

    for copy in base_copies:
        copy.wait()
    base_noise_copies[0].wait()

    @pl.loop(0, TILES)
    def _(t):
        for x in range(CHUNKS):
            lanes = pl.ds(x * LANES, LANES)
            p, r = divmod(x, ROWS)
            mat = matrix(lambda c: tile_grad[t, p, c, pl.ds(r, 1), :], jnp.ones((1, LANES), F32))
            state = [base[t, c, :, lanes] for c in range(3)]
            noise = [base_noise[t, c, :, lanes] for c in range(3)]
            moved = advance(mat, state, noise)
            for c in range(3):
                drifted[t, c, :, lanes] = moved[c]
            own_sums[t, 0, pl.ds(x, 1), :] = row_sum(inner(state, state))
            own_sums[t, 1, pl.ds(x, 1), :] = row_sum(inner(state, moved))
            own_sums[t, 2, pl.ds(x, 1), :] = row_sum(inner(moved, moved))

    @pl.loop(0, n_gy)
    def _(k):
        tile = lax.rem(helper[lax.rem(gy + k, n_gy)], TILES)
        own_send[k] = own_sums[tile]

    own_copies = send_all(
        lambda k: own_send.at[k],
        lambda k: own_recv.at[k],
        lambda k: own_send_sem.at[k],
        lambda k: own_recv_sem.at[k],
    )
    own_recv[0] = own_send[0]

    for copy in extra_copies:
        copy.wait_recv()
    for t in range(TILES):
        slot, hit = slots[t]
        count = jnp.full((CHUNKS, LANES), counts[t], jnp.int32).astype(F32)
        total = own_sums[t, 0] + jnp.where(hit == 1, extra_recv[slot], 0.0)
        rate = relaxation(total, count)
        relax[t] = rate
        own = own_sums[t, 2] - rate * (2.0 * own_sums[t, 1] - rate * own_sums[t, 0])
        for p in range(PARTS):
            own_total[t, p] = part_of(own, p)

    @pl.loop(0, TILES)
    def _(t):
        for x in range(CHUNKS):
            lanes = pl.ds(x * LANES, LANES)
            rate = wide(relax[t, pl.ds(x, 1), :])
            for c in range(3):
                base[t, c, :, lanes] = drifted[t, c, :, lanes] - rate * base[t, c, :, lanes]

    for copy in own_copies:
        copy.wait_recv()
    sums = [own_recv[my_slot, m] for m in range(3)]
    rate = relaxation(sums[0] + extra_sum[...], 256.0)
    helper_relax[...] = rate
    helper_total[...] = sums[2] - rate * (2.0 * sums[1] - rate * sums[0])

    for copy in extra_noise_copies:
        copy.wait()
    moment_copies = []
    for p in range(PARTS):
        for copy in grad_copies[p]:
            copy.wait_recv()

        @pl.loop(0, ROWS)
        def _(r):
            x = p * ROWS + r
            lanes = pl.ds(pl.multiple_of(x * LANES, LANES), LANES)
            mat = matrix(
                lambda c: grad_recv[p][my_slot, c, pl.ds(r, 1), :],
                1.0 - helper_relax[pl.ds(x, 1), :],
            )
            total = jnp.zeros((8, LANES), F32)
            for f in range(EXTRA // GROUP):
                fields = pl.ds(f * GROUP, GROUP)
                state = [extra[c, fields, lanes] for c in range(3)]
                noise = [extra_noise[0, c, fields, lanes] for c in range(3)]
                state = advance(mat, state, noise)
                for c in range(3):
                    extra[c, fields, lanes] = state[c]
                total = total + inner(state, state)
            row_total[pl.ds(x, 1), :] = row_sum(total)

        here = row_total[pl.ds(p * ROWS, ROWS), :]
        moment_recv[0, p, 6] = here
        helper_relax[pl.ds(p * ROWS, ROWS), :] = relaxation(
            here + helper_total[pl.ds(p * ROWS, ROWS), :], 256.0
        )

        @pl.loop(0, ROWS)
        def _(r):
            x = p * ROWS + r
            lanes = pl.ds(pl.multiple_of(x * LANES, LANES), LANES)
            mat = matrix(
                lambda c: grad_recv[p][my_slot, c, pl.ds(r, 1), :],
                1.0 - helper_relax[pl.ds(x, 1), :],
            )
            totals = [jnp.zeros((8, LANES), F32) for _ in range(6)]
            for f in range(EXTRA // GROUP):
                fields = pl.ds(f * GROUP, GROUP)
                state = [extra[c, fields, lanes] for c in range(3)]
                noise = [extra_noise[1, c, fields, lanes] for c in range(3)]
                state = advance(mat, state, noise)
                for c in range(3):
                    extra[c, fields, lanes] = state[c]
                totals = [u + v for u, v in zip(totals, products(state))]
            for m in range(6):
                moment_recv[0, p, m, pl.ds(r, 1), :] = row_sum(totals[m])

        moment_copies.append(
            send_all(
                lambda k: moment_recv.at[0, p],
                lambda k: moment_recv.at[k, p],
                lambda k: moment_send_sem.at[p, k],
                lambda k: moment_recv_sem.at[p, k],
            )
        )

    base_noise_copies[1].wait()
    for copies in (halo_copies, extra_copies, own_copies, *grad_copies):
        for copy in copies:
            copy.wait_send()
    for copies in moment_copies:
        for copy in copies:
            copy.wait_recv()
            copy.wait_send()


def finish_kernel(
    n_gy,
    counts,
    helper,
    start,
    extra,
    noise,
    tile_grad,
    own_total,
    moment_recv,
    base_out,
    extra_out,
    stress_out,
    base,
    stress,
    staged,
    relax,
    moment,
    tile_sem,
    out_sem,
):
    gy = lax.axis_index("gy")
    extra_copy = pltpu.make_async_copy(extra, extra_out, out_sem.at[0])
    extra_copy.start()

    @pl.loop(0, TILES)
    def _(t):
        slot, hit = helper_slots(helper, gy, n_gy, t)
        heavy = hit == 1
        count = jnp.full((ROWS, LANES), counts[t], jnp.int32).astype(F32)
        for p in range(PARTS):
            total = own_total[t, p] + jnp.where(heavy, moment_recv[slot, p, 6], 0.0)
            relax[p] = relaxation(total, count)
        for x in range(CHUNKS):
            lanes = pl.ds(x * LANES, LANES)
            p, r = divmod(x, ROWS)
            mat = matrix(
                lambda c: tile_grad[t, p, c, pl.ds(r, 1), :], 1.0 - relax[p, pl.ds(r, 1), :]
            )
            state = [start[t, c, :, lanes] for c in range(3)]
            state = advance(mat, state, [noise[t, c, :, lanes] for c in range(3)])
            for c in range(3):
                base[t, c, :, lanes] = state[c]
            for m, total in enumerate(products(state)):
                moment[p, m, pl.ds(r, 1), :] = row_sum(total)
        pltpu.make_async_copy(base.at[t], base_out.at[t], tile_sem.at[t]).start()
        for p in range(PARTS):
            second = [
                (moment[p, m] + jnp.where(heavy, moment_recv[slot, p, m], 0.0)) / count
                for m in range(6)
            ]
            trace = second[0] + second[1] + second[2]
            stretch = 1.0 / (1.0 - trace / max_extension)
            for m in range(6):
                value = (stretch * second[m] - (1.0 if m < 3 else 0.0)) / weissenberg
                for r in range(ROWS):
                    staged[m, p * ROWS + r, pl.ds(t, 1), :] = value[r : r + 1]

    for m in range(6):
        for x in range(CHUNKS):
            stress[m, :, pl.ds(x * LANES, LANES)] = staged[m, x]
    stress_copy = pltpu.make_async_copy(stress, stress_out, out_sem.at[1])
    stress_copy.start()
    for t in range(TILES):
        pltpu.make_async_copy(base.at[t], base_out.at[t], tile_sem.at[t]).wait()
    extra_copy.wait()
    stress_copy.wait()


def hold(array):
    return pltpu.with_memory_space_constraint(array, pltpu.HBM)


def solution(mesh):
    n_gx, n_gy = mesh.shape["gx"], mesh.shape["gy"]

    def per_device(
        velocity,
        wall_cells,
        tile_counts,
        helper_tile,
        base_fields,
        extra_fields,
        base_noise,
        extra_noise,
    ):
        hbm = pl.BlockSpec(memory_space=pltpu.HBM)
        vmem = pl.BlockSpec(memory_space=pltpu.VMEM)
        smem = pl.BlockSpec(memory_space=pltpu.SMEM)
        dma = pltpu.SemaphoreType.DMA
        counts = hold(tile_counts.reshape(TILES))
        helper = hold(helper_tile.reshape(n_gy))
        grad_buffer = pltpu.VMEM((n_gy, 9, ROWS, LANES), F32)
        passed = pl.pallas_call(
            functools.partial(exchange_kernel, n_gx, n_gy),
            out_shape=(
                jax.ShapeDtypeStruct((TILES, 3, BASE, CELLS), F32),
                jax.ShapeDtypeStruct((3, EXTRA, CELLS), F32),
                jax.ShapeDtypeStruct((TILES, 3, BASE, CELLS), jnp.bfloat16),
                jax.ShapeDtypeStruct((TILES, PARTS, 9, ROWS, LANES), F32),
                jax.ShapeDtypeStruct((TILES, PARTS, ROWS, LANES), F32),
                jax.ShapeDtypeStruct((n_gy, PARTS, 7, ROWS, LANES), F32),
            ),
            in_specs=[smem] * 2 + [hbm] * 6,
            out_specs=(vmem,) * 6,
            scratch_shapes=[
                pltpu.VMEM((3, 8, 8, LANES), F32),
                pltpu.VMEM((8, 8, LANES), jnp.int32),
                pltpu.VMEM((TILES, 3, BASE, CELLS), F32),
                pltpu.VMEM((TILES, 3, BASE, CELLS), jnp.bfloat16),
                pltpu.VMEM((STEPS, 3, EXTRA, CELLS), jnp.bfloat16),
                pltpu.VMEM((2, 3, 8, LANES), F32),
                pltpu.VMEM((2, 3, 8, LANES), F32),
                pltpu.VMEM((2, 3, 8, LANES), F32),
                pltpu.VMEM((TILES, 3, CHUNKS, LANES), F32),
                pltpu.VMEM((CHUNKS, LANES), F32),
                pltpu.VMEM((n_gy, CHUNKS, LANES), F32),
                pltpu.VMEM((n_gy, 3, CHUNKS, LANES), F32),
                pltpu.VMEM((n_gy, 3, CHUNKS, LANES), F32),
                pltpu.VMEM((CHUNKS, LANES), F32),
                pltpu.VMEM((CHUNKS, LANES), F32),
                pltpu.VMEM((CHUNKS, LANES), F32),
                pltpu.VMEM((TILES, CHUNKS, LANES), F32),
                *[grad_buffer] * (2 * PARTS),
                dma((7,)),
                dma((TILES,)),
                dma((4,)),
                dma((4,)),
                dma((n_gy,)),
                dma((n_gy,)),
                dma((n_gy,)),
                dma((n_gy,)),
                dma((PARTS, n_gy)),
                dma((PARTS, n_gy)),
                dma((PARTS, n_gy)),
                dma((PARTS, n_gy)),
            ],
            compiler_params=pltpu.CompilerParams(
                collective_id=0, has_side_effects=True, vmem_limit_bytes=40 << 20
            ),
        )(
            counts,
            helper,
            hold(velocity),
            hold(wall_cells),
            hold(base_fields.reshape(TILES, 3, BASE, CELLS)),
            hold(extra_fields.reshape(3, EXTRA, CELLS)),
            hold(base_noise.reshape(TILES, STEPS, 3, BASE, CELLS)),
            hold(extra_noise.reshape(STEPS, 3, EXTRA, CELLS)),
        )
        base_out, extra_out, stress_out = pl.pallas_call(
            functools.partial(finish_kernel, n_gy),
            out_shape=(
                jax.ShapeDtypeStruct((TILES, 3, BASE, CELLS), F32),
                jax.ShapeDtypeStruct((3, EXTRA, CELLS), F32),
                jax.ShapeDtypeStruct((6, TILES, CELLS), F32),
            ),
            in_specs=[smem] * 2 + [vmem] * 6,
            out_specs=(hbm,) * 3,
            scratch_shapes=[
                pltpu.VMEM((TILES, 3, BASE, CELLS), F32),
                pltpu.VMEM((6, TILES, CELLS), F32),
                pltpu.VMEM((6, CHUNKS, TILES, LANES), F32),
                pltpu.VMEM((PARTS, ROWS, LANES), F32),
                pltpu.VMEM((PARTS, 6, ROWS, LANES), F32),
                dma((TILES,)),
                dma((2,)),
            ],
            compiler_params=pltpu.CompilerParams(vmem_limit_bytes=40 << 20),
        )(counts, helper, *passed)
        return base_out[None, None], extra_out[None, None], stress_out.transpose(1, 0, 2)[None, None]

    in_specs = (
        P(None, "gx", "gy", None),
        P("gx", "gy", None),
        P("gx", "gy", None),
        P("gx", None),
        P("gx", "gy", None, None, None, None),
        P("gx", "gy", None, None, None),
        P("gx", "gy", None, None, None, None, None),
        P("gx", "gy", None, None, None, None),
    )
    out_specs = (
        P("gx", "gy", None, None, None, None),
        P("gx", "gy", None, None, None),
        P("gx", "gy", None, None, None),
    )
    return jax.shard_map(
        per_device, mesh=mesh, in_specs=in_specs, out_specs=out_specs, check_vma=False
    )
```

```python
import functools

import jax
import jax.numpy as jnp
from jax import lax
from jax.experimental import pallas as pl
from jax.experimental.pallas import tpu as pltpu
from jax.sharding import PartitionSpec as P

MESH = pl.DeviceIdType.MESH
F32 = jnp.float32

STEPS = 2
TILES = 8
CELLS = 1024
LANES = 128
CHUNKS = CELLS // LANES
BASE = 32
EXTRA = 224
GROUP = 32
PARTS = 2
ROWS = CHUNKS // PARTS

time_step = 0.05
weissenberg = 0.25
max_extension = 50.0
noise_scale = (time_step / weissenberg) ** 0.5
relax_scale = time_step * (0.5 / weissenberg)
component_pairs = ((0, 0), (1, 1), (2, 2), (0, 1), (0, 2), (1, 2))


def wide(row):
    return jnp.broadcast_to(row, (GROUP, LANES))


def matrix(grad_row, keep_row):
    keep = wide(keep_row)
    rows = []
    for a in range(3):
        row = [wide(grad_row(3 * a + b)) for b in range(3)]
        row[a] = row[a] + keep
        rows.append(row)
    return rows


def advance(mat, state, noise):
    return [
        mat[a][0] * state[0]
        + mat[a][1] * state[1]
        + mat[a][2] * state[2]
        + noise_scale * noise[a].astype(F32)
        for a in range(3)
    ]


def fold(block):
    out = block[:8]
    for k in range(1, block.shape[0] // 8):
        out = out + block[8 * k : 8 * k + 8]
    return out


def inner(left, right):
    return fold(left[0] * right[0] + left[1] * right[1] + left[2] * right[2])


def products(state):
    return [fold(state[a] * state[b]) for a, b in component_pairs]


def row_sum(block):
    return jnp.sum(block, axis=0, keepdims=True)


def relaxation(total, count):
    return relax_scale * (1.0 / (1.0 - total / count / max_extension))


def helper_slots(helper, gy, n_gy, t):
    slot, hit = jnp.int32(0), jnp.int32(0)
    for h in range(n_gy):
        match = helper[h] == gy * TILES + t
        slot = jnp.where(match, lax.rem(gy - h + n_gy, n_gy), slot)
        hit = jnp.where(match, 1, hit)
    return slot, hit


def swap_blocks(regs, block):
    for bit in (1, 2, 4):
        upper = (block & bit) != 0
        new = list(regs)
        for i in range(8):
            if i & bit:
                continue
            j = i | bit
            new[i] = jnp.where(upper, pltpu.roll(regs[j], 16 * bit, 1), regs[i])
            new[j] = jnp.where(upper, regs[j], pltpu.roll(regs[i], LANES - 16 * bit, 1))
        regs = new
    return regs


def gradient(velocity, z_edge, fluid, y_edge, x_edge, sub, lane):
    deep = lane % 16

    def turn(value, shift):
        shift = shift % LANES
        return pltpu.roll(value, shift, 1) if shift else value

    grads = []
    for a in range(3):
        v = velocity[a]
        low = jnp.broadcast_to(x_edge[a : a + 1], (8, LANES))
        high = jnp.broadcast_to(x_edge[3 + a : 4 + a], (8, LANES))
        before = jnp.where(sub == 0, low, pltpu.roll(v, 1, 0))
        after = jnp.where(sub == 7, high, pltpu.roll(v, 7, 0))
        grads.append((after - before) * fluid)
        before = jnp.where(lane < 16, turn(y_edge, -16 * a), turn(v, 16))
        after = jnp.where(lane >= 112, turn(y_edge, 16 * (4 - a)), turn(v, -16))
        grads.append((after - before) * fluid)
        before = jnp.where(deep == 0, turn(z_edge, -a), turn(v, 1))
        after = jnp.where(deep == 15, turn(z_edge, a), turn(v, -1))
        grads.append((after - before) * fluid)
    return grads


def exchange_kernel(
    n_gx,
    n_gy,
    counts_hbm,
    helper_hbm,
    vel_hbm,
    wall_hbm,
    base_hbm,
    extra_hbm,
    base_noise_hbm,
    extra_noise_hbm,
    base,
    extra,
    late_noise,
    tile_grad,
    own_total,
    moment_recv,
    counts,
    helper,
    vel,
    wall,
    base_noise,
    extra_noise,
    y_send,
    x_halo,
    y_halo,
    second,
    flow_own,
    flow_send,
    flow_recv,
    sum_own,
    extra_sum,
    sum_send,
    sum_recv,
    edge_own,
    edge_send,
    edge_recv,
    helper_grad,
    helper_relax,
    helper_total,
    row_total,
    relax,
    in_sem,
    tile_sem,
    halo_send_sem,
    halo_recv_sem,
    flow_send_sem,
    flow_recv_sem,
    sum_send_sem,
    sum_recv_sem,
    edge_send_sem,
    edge_recv_sem,
    moment_send_sem,
    moment_recv_sem,
):
    gx = lax.axis_index("gx")
    gy = lax.axis_index("gy")
    up_x, down_x = lax.rem(gx + 1, n_gx), lax.rem(gx + n_gx - 1, n_gx)
    up_y, down_y = lax.rem(gy + 1, n_gy), lax.rem(gy + n_gy - 1, n_gy)

    barrier = pltpu.get_barrier_semaphore()
    for k in range(1, n_gy):
        peer = lax.rem(gy + k, n_gy)
        pl.semaphore_signal(barrier, inc=1, device_id=(gx, peer), device_id_type=MESH)
    for peer in (up_x, down_x):
        pl.semaphore_signal(barrier, inc=1, device_id=(peer, gy), device_id_type=MESH)

    vel_copy = pltpu.make_async_copy(vel_hbm, vel, in_sem.at[0])
    wall_copy = pltpu.make_async_copy(wall_hbm, wall, in_sem.at[1])
    helper_copy = pltpu.make_async_copy(helper_hbm, helper, in_sem.at[7])
    counts_copy = pltpu.make_async_copy(counts_hbm, counts, in_sem.at[8])
    extra_copy = pltpu.make_async_copy(extra_hbm, extra, in_sem.at[2])
    base_copies = [
        pltpu.make_async_copy(base_hbm.at[t], base.at[t], tile_sem.at[t]) for t in range(TILES)
    ]
    base_noise_copies = [
        pltpu.make_async_copy(base_noise_hbm.at[:, 0], base_noise, in_sem.at[3]),
        pltpu.make_async_copy(base_noise_hbm.at[:, 1], late_noise, in_sem.at[4]),
    ]
    extra_noise_copies = [
        pltpu.make_async_copy(extra_noise_hbm.at[s], extra_noise.at[s], in_sem.at[5 + s])
        for s in range(STEPS)
    ]
    vel_copy.start()
    wall_copy.start()
    helper_copy.start()
    counts_copy.start()
    for copy in base_copies:
        copy.start()
    base_noise_copies[0].start()
    extra_copy.start()
    extra_noise_copies[0].start()
    extra_noise_copies[1].start()
    base_noise_copies[1].start()

    def send_all(src_of, dst_of, send_sem, recv_sem):
        copies = [
            pltpu.make_async_remote_copy(
                src_ref=src_of(k),
                dst_ref=dst_of(k),
                send_sem=send_sem(k),
                recv_sem=recv_sem(k),
                device_id=(gx, lax.rem(gy + k, n_gy)),
                device_id_type=MESH,
            )
            for k in range(1, n_gy)
        ]
        for copy in copies:
            copy.start()
        return copies

    def wanted(k):
        return lax.rem(helper[lax.rem(gy + k, n_gy)], TILES)

    sub = lax.broadcasted_iota(jnp.int32, (8, LANES), 0)
    lane = lax.broadcasted_iota(jnp.int32, (8, LANES), 1)
    block = lane // 16
    deep = lane % 16
    vel_copy.wait()
    for c in range(3):
        y_send[0, c] = vel[c, :, 7, :]
        y_send[1, c] = vel[c, :, 0, :]
    x_halo[6:] = jnp.zeros((2, 8, LANES), F32)
    flow = [swap_blocks([vel[a, :, y, :] for y in range(8)], block) for a in range(3)]
    for t in range(TILES):
        z_edge = jnp.zeros((8, LANES), F32)
        for a in range(3):
            if t > 0:
                z_edge = jnp.where(deep == a, pltpu.roll(flow[a][t - 1], 113 + a, 1), z_edge)
            if t < TILES - 1:
                z_edge = jnp.where(deep == 15 - a, pltpu.roll(flow[a][t + 1], 15 - a, 1), z_edge)
            flow_own[t, a] = flow[a][t]
        flow_own[t, 3] = z_edge
    wall_copy.wait()
    fluid = swap_blocks(
        [jnp.where(wall[:, y, :] == 0, 0.5 * time_step, 0.0).astype(F32) for y in range(8)], block
    )
    for t in range(TILES):
        flow_own[t, 4] = fluid[t]
    helper_copy.wait()
    counts_copy.wait()

    @pl.loop(0, n_gy)
    def _(k):
        flow_send[k] = flow_own[wanted(k)]

    pl.semaphore_wait(barrier, n_gy + 1)

    halo_copies = [
        pltpu.make_async_remote_copy(
            src_ref=src,
            dst_ref=dst,
            send_sem=halo_send_sem.at[i],
            recv_sem=halo_recv_sem.at[i],
            device_id=device,
            device_id_type=MESH,
        )
        for i, (src, dst, device) in enumerate(
            (
                (vel.at[:, 7], x_halo.at[0:3], (up_x, gy)),
                (vel.at[:, 0], x_halo.at[3:6], (down_x, gy)),
                (y_send.at[0], y_halo.at[0:3], (gx, up_y)),
                (y_send.at[1], y_halo.at[3:6], (gx, down_y)),
            )
        )
    ]
    for copy in halo_copies:
        copy.start()
    flow_copies = send_all(
        lambda k: flow_send.at[k],
        lambda k: flow_recv.at[k],
        lambda k: flow_send_sem.at[k],
        lambda k: flow_recv_sem.at[k],
    )
    flow_recv[0] = flow_send[0]

    my_slot = lax.rem(gy - helper[gy] // TILES + n_gy, n_gy)
    slots = [helper_slots(helper, gy, n_gy, t) for t in range(TILES)]

    for copy in base_copies:
        copy.wait()
    base_noise_copies[0].wait()

    @pl.loop(0, TILES)
    def _(t):
        for x in range(CHUNKS):
            lanes = pl.ds(x * LANES, LANES)
            state = [base[t, c, :, lanes] for c in range(3)]
            noise = [base_noise[t, c, :, lanes].astype(F32) for c in range(3)]
            for m, total in enumerate(products(state)):
                second[t, m, pl.ds(x, 1), :] = row_sum(total)
            for a in range(3):
                for b in range(3):
                    second[t, 6 + 3 * a + b, pl.ds(x, 1), :] = row_sum(fold(state[a] * noise[b]))
            second[t, 15, pl.ds(x, 1), :] = row_sum(inner(noise, noise))

    for t in range(TILES):
        sum_own[t] = second[t, 0] + second[t, 1] + second[t, 2]

    extra_copy.wait()

    @pl.loop(0, CHUNKS)
    def _(x):
        lanes = pl.ds(pl.multiple_of(x * LANES, LANES), LANES)
        total = jnp.zeros((8, LANES), F32)
        for f in range(EXTRA // GROUP):
            state = [extra[c, pl.ds(f * GROUP, GROUP), lanes] for c in range(3)]
            total = total + inner(state, state)
        extra_sum[pl.ds(x, 1), :] = row_sum(total)

    @pl.loop(0, n_gy)
    def _(k):
        sum_send[k, 0] = sum_own[wanted(k)]
        sum_send[k, 1] = extra_sum[...]

    sum_copies = send_all(
        lambda k: sum_send.at[k],
        lambda k: sum_recv.at[k],
        lambda k: sum_send_sem.at[k],
        lambda k: sum_recv_sem.at[k],
    )
    sum_recv[0] = sum_send[0]

    for copy in halo_copies:
        copy.wait_recv()
    low = jnp.where(gx > 0, 1.0, 0.0)
    high = jnp.where(gx < n_gx - 1, 1.0, 0.0)
    inside = jnp.where(sub < 3, low, high)
    x_edges = swap_blocks([x_halo[:, y, :] * inside for y in range(8)], block)
    sides = [jnp.where(gy > 0, y_halo[a], 0.0) for a in range(3)]
    sides += [jnp.where(gy < n_gy - 1, y_halo[3 + a], 0.0) for a in range(3)]
    sides += [jnp.zeros((8, LANES), F32)] * 2
    y_edges = swap_blocks(sides, block)
    for t in range(TILES):
        edge_own[t, 0] = y_edges[t]
        edge_own[t, 1] = x_edges[t]

    @pl.loop(0, TILES)
    def _(t):
        grads = gradient(
            [flow_own[t, a] for a in range(3)],
            flow_own[t, 3],
            flow_own[t, 4],
            edge_own[t, 0],
            edge_own[t, 1],
            sub,
            lane,
        )
        for c in range(9):
            tile_grad[t, c] = grads[c]
        mat = [[grads[3 * a + b] + (1.0 if a == b else 0.0) for b in range(3)] for a in range(3)]
        pairs = {}
        for m, (a, b) in enumerate(component_pairs):
            pairs[a, b] = pairs[b, a] = second[t, m]
        cross = [[second[t, 6 + 3 * a + b] for b in range(3)] for a in range(3)]
        once = noise_scale * (cross[0][0] + cross[1][1] + cross[2][2])
        twice = (noise_scale * noise_scale) * second[t, 15]
        for a in range(3):
            for b in range(3):
                inner_row = (
                    mat[a][0] * pairs[0, b] + mat[a][1] * pairs[1, b] + mat[a][2] * pairs[2, b]
                )
                once = once + (mat[a][b] * pairs[a, b])
                twice = twice + mat[a][b] * (inner_row + (2.0 * noise_scale) * cross[b][a])
        edge_own[t, 2] = once
        edge_own[t, 3] = twice

    @pl.loop(0, n_gy)
    def _(k):
        edge_send[k] = edge_own[wanted(k)]

    edge_copies = send_all(
        lambda k: edge_send.at[k],
        lambda k: edge_recv.at[k],
        lambda k: edge_send_sem.at[k],
        lambda k: edge_recv_sem.at[k],
    )
    edge_recv[0] = edge_send[0]

    for copy in sum_copies:
        copy.wait_recv()
    for t in range(TILES):
        slot, hit = slots[t]
        count = jnp.full((CHUNKS, LANES), counts[t], jnp.int32).astype(F32)
        total = sum_own[t] + jnp.where(hit == 1, sum_recv[slot, 1], 0.0)
        rate = relaxation(total, count)
        relax[t] = 1.0 - rate
        own_total[t] = edge_own[t, 3] - rate * (2.0 * edge_own[t, 2] - rate * sum_own[t])

    @pl.loop(0, TILES)
    def _(t):
        for x in range(CHUNKS):
            lanes = pl.ds(x * LANES, LANES)
            mat = matrix(lambda c: tile_grad[t, c, pl.ds(x, 1), :], relax[t, pl.ds(x, 1), :])
            state = [base[t, c, :, lanes] for c in range(3)]
            state = advance(mat, state, [base_noise[t, c, :, lanes] for c in range(3)])
            for c in range(3):
                base[t, c, :, lanes] = state[c]

    for copies in (flow_copies, edge_copies):
        for copy in copies:
            copy.wait_recv()
    grads = gradient(
        [flow_recv[my_slot, a] for a in range(3)],
        flow_recv[my_slot, 3],
        flow_recv[my_slot, 4],
        edge_recv[my_slot, 0],
        edge_recv[my_slot, 1],
        sub,
        lane,
    )
    for c in range(9):
        helper_grad[c] = grads[c]
    first = sum_recv[my_slot, 0]
    rate = relaxation(first + extra_sum[...], 256.0)
    helper_relax[...] = 1.0 - rate
    helper_total[...] = edge_recv[my_slot, 3] - rate * (2.0 * edge_recv[my_slot, 2] - rate * first)

    for copy in extra_noise_copies:
        copy.wait()
    moment_copies = []
    for p in range(PARTS):

        @pl.loop(0, ROWS)
        def _(r):
            x = p * ROWS + r
            lanes = pl.ds(pl.multiple_of(x * LANES, LANES), LANES)
            mat = matrix(
                lambda c: helper_grad[c, pl.ds(x, 1), :], helper_relax[pl.ds(x, 1), :]
            )
            total = jnp.zeros((8, LANES), F32)
            for f in range(EXTRA // GROUP):
                fields = pl.ds(f * GROUP, GROUP)
                state = [extra[c, fields, lanes] for c in range(3)]
                noise = [extra_noise[0, c, fields, lanes] for c in range(3)]
                state = advance(mat, state, noise)
                for c in range(3):
                    extra[c, fields, lanes] = state[c]
                total = total + inner(state, state)
            row_total[pl.ds(x, 1), :] = row_sum(total)

        rows = pl.ds(p * ROWS, ROWS)
        here = row_total[rows, :]
        moment_recv[0, p, 6] = here
        helper_relax[rows, :] = 1.0 - relaxation(here + helper_total[rows, :], 256.0)

        @pl.loop(0, ROWS)
        def _(r):
            x = p * ROWS + r
            lanes = pl.ds(pl.multiple_of(x * LANES, LANES), LANES)
            mat = matrix(
                lambda c: helper_grad[c, pl.ds(x, 1), :], helper_relax[pl.ds(x, 1), :]
            )
            totals = [jnp.zeros((8, LANES), F32) for _ in range(6)]
            for f in range(EXTRA // GROUP):
                fields = pl.ds(f * GROUP, GROUP)
                state = [extra[c, fields, lanes] for c in range(3)]
                noise = [extra_noise[1, c, fields, lanes] for c in range(3)]
                state = advance(mat, state, noise)
                for c in range(3):
                    extra[c, fields, lanes] = state[c]
                totals = [u + v for u, v in zip(totals, products(state))]
            for m in range(6):
                moment_recv[0, p, m, pl.ds(r, 1), :] = row_sum(totals[m])

        moment_copies.append(
            send_all(
                lambda k: moment_recv.at[0, p],
                lambda k: moment_recv.at[k, p],
                lambda k: moment_send_sem.at[p, k],
                lambda k: moment_recv_sem.at[p, k],
            )
        )

    base_noise_copies[1].wait()
    for copies in (halo_copies, flow_copies, sum_copies, edge_copies):
        for copy in copies:
            copy.wait_send()
    for copies in moment_copies:
        for copy in copies:
            copy.wait_recv()
            copy.wait_send()


def finish_kernel(
    n_gy,
    counts_hbm,
    helper_hbm,
    start,
    extra,
    noise,
    tile_grad,
    own_total,
    moment_recv,
    base_out,
    extra_out,
    stress_out,
    counts,
    helper,
    base,
    stress,
    staged,
    relax,
    moment,
    tile_sem,
    out_sem,
):
    gy = lax.axis_index("gy")
    helper_copy = pltpu.make_async_copy(helper_hbm, helper, out_sem.at[2])
    counts_copy = pltpu.make_async_copy(counts_hbm, counts, out_sem.at[3])
    extra_copy = pltpu.make_async_copy(extra, extra_out, out_sem.at[0])
    helper_copy.start()
    counts_copy.start()
    extra_copy.start()
    helper_copy.wait()
    counts_copy.wait()

    @pl.loop(0, TILES)
    def _(t):
        slot, hit = helper_slots(helper, gy, n_gy, t)
        heavy = hit == 1
        count = jnp.full((ROWS, LANES), counts[t], jnp.int32).astype(F32)
        for p in range(PARTS):
            total = own_total[t, pl.ds(p * ROWS, ROWS), :] + jnp.where(heavy, moment_recv[slot, p, 6], 0.0)
            relax[p] = relaxation(total, count)
        for x in range(CHUNKS):
            lanes = pl.ds(x * LANES, LANES)
            p, r = divmod(x, ROWS)
            mat = matrix(
                lambda c: tile_grad[t, c, pl.ds(x, 1), :], 1.0 - relax[p, pl.ds(r, 1), :]
            )
            state = [start[t, c, :, lanes] for c in range(3)]
            state = advance(mat, state, [noise[t, c, :, lanes] for c in range(3)])
            for c in range(3):
                base[t, c, :, lanes] = state[c]
            for m, total in enumerate(products(state)):
                moment[p, m, pl.ds(r, 1), :] = row_sum(total)
        pltpu.make_async_copy(base.at[t], base_out.at[t], tile_sem.at[t]).start()
        for p in range(PARTS):
            second = [
                (moment[p, m] + jnp.where(heavy, moment_recv[slot, p, m], 0.0)) / count
                for m in range(6)
            ]
            trace = second[0] + second[1] + second[2]
            stretch = 1.0 / (1.0 - trace / max_extension)
            for m in range(6):
                value = (stretch * second[m] - (1.0 if m < 3 else 0.0)) / weissenberg
                for r in range(ROWS):
                    staged[m, p * ROWS + r, pl.ds(t, 1), :] = value[r : r + 1]

    for m in range(6):
        for x in range(CHUNKS):
            stress[m, :, pl.ds(x * LANES, LANES)] = staged[m, x]
    stress_copy = pltpu.make_async_copy(stress, stress_out, out_sem.at[1])
    stress_copy.start()
    for t in range(TILES):
        pltpu.make_async_copy(base.at[t], base_out.at[t], tile_sem.at[t]).wait()
    extra_copy.wait()
    stress_copy.wait()


def hold(array):
    return pltpu.with_memory_space_constraint(array, pltpu.HBM)


def solution(mesh):
    n_gx, n_gy = mesh.shape["gx"], mesh.shape["gy"]

    def per_device(
        velocity,
        wall_cells,
        tile_counts,
        helper_tile,
        base_fields,
        extra_fields,
        base_noise,
        extra_noise,
    ):
        hbm = pl.BlockSpec(memory_space=pltpu.HBM)
        vmem = pl.BlockSpec(memory_space=pltpu.VMEM)
        dma = pltpu.SemaphoreType.DMA
        counts = hold(tile_counts.reshape(TILES))
        helper = hold(helper_tile.reshape(n_gy))

        def block(*lead):
            return pltpu.VMEM((*lead, CHUNKS, LANES), F32)

        passed = pl.pallas_call(
            functools.partial(exchange_kernel, n_gx, n_gy),
            out_shape=(
                jax.ShapeDtypeStruct((TILES, 3, BASE, CELLS), F32),
                jax.ShapeDtypeStruct((3, EXTRA, CELLS), F32),
                jax.ShapeDtypeStruct((TILES, 3, BASE, CELLS), jnp.bfloat16),
                jax.ShapeDtypeStruct((TILES, 9, CHUNKS, LANES), F32),
                jax.ShapeDtypeStruct((TILES, CHUNKS, LANES), F32),
                jax.ShapeDtypeStruct((n_gy, PARTS, 7, ROWS, LANES), F32),
            ),
            in_specs=[hbm] * 8,
            out_specs=(vmem,) * 6,
            scratch_shapes=[
                pltpu.SMEM((TILES,), jnp.int32),
                pltpu.SMEM((n_gy,), jnp.int32),
                block(3, 8),
                pltpu.VMEM((8, 8, LANES), jnp.int32),
                pltpu.VMEM((TILES, 3, BASE, CELLS), jnp.bfloat16),
                pltpu.VMEM((STEPS, 3, EXTRA, CELLS), jnp.bfloat16),
                block(2, 3),
                block(8),
                block(6),
                block(TILES, 16),
                block(TILES, 5),
                block(n_gy, 5),
                block(n_gy, 5),
                block(TILES),
                block(),
                block(n_gy, 2),
                block(n_gy, 2),
                block(TILES, 4),
                block(n_gy, 4),
                block(n_gy, 4),
                block(9),
                block(),
                block(),
                block(),
                block(TILES),
                dma((9,)),
                dma((TILES,)),
                dma((4,)),
                dma((4,)),
                dma((n_gy,)),
                dma((n_gy,)),
                dma((n_gy,)),
                dma((n_gy,)),
                dma((n_gy,)),
                dma((n_gy,)),
                dma((PARTS, n_gy)),
                dma((PARTS, n_gy)),
            ],
            compiler_params=pltpu.CompilerParams(
                collective_id=0, has_side_effects=True, vmem_limit_bytes=40 << 20
            ),
        )(
            counts,
            helper,
            hold(velocity),
            hold(wall_cells),
            hold(base_fields.reshape(TILES, 3, BASE, CELLS)),
            hold(extra_fields.reshape(3, EXTRA, CELLS)),
            hold(base_noise.reshape(TILES, STEPS, 3, BASE, CELLS)),
            hold(extra_noise.reshape(STEPS, 3, EXTRA, CELLS)),
        )
        base_out, extra_out, stress_out = pl.pallas_call(
            functools.partial(finish_kernel, n_gy),
            out_shape=(
                jax.ShapeDtypeStruct((TILES, 3, BASE, CELLS), F32),
                jax.ShapeDtypeStruct((3, EXTRA, CELLS), F32),
                jax.ShapeDtypeStruct((6, TILES, CELLS), F32),
            ),
            in_specs=[hbm] * 2 + [vmem] * 6,
            out_specs=(hbm,) * 3,
            scratch_shapes=[
                pltpu.SMEM((TILES,), jnp.int32),
                pltpu.SMEM((n_gy,), jnp.int32),
                pltpu.VMEM((TILES, 3, BASE, CELLS), F32),
                pltpu.VMEM((6, TILES, CELLS), F32),
                pltpu.VMEM((6, CHUNKS, TILES, LANES), F32),
                pltpu.VMEM((PARTS, ROWS, LANES), F32),
                pltpu.VMEM((PARTS, 6, ROWS, LANES), F32),
                dma((TILES,)),
                dma((4,)),
            ],
            compiler_params=pltpu.CompilerParams(vmem_limit_bytes=40 << 20),
        )(counts, helper, *passed)
        return base_out[None, None], extra_out[None, None], stress_out.transpose(1, 0, 2)[None, None]

    in_specs = (
        P(None, "gx", "gy", None),
        P("gx", "gy", None),
        P("gx", "gy", None),
        P("gx", None),
        P("gx", "gy", None, None, None, None),
        P("gx", "gy", None, None, None),
        P("gx", "gy", None, None, None, None, None),
        P("gx", "gy", None, None, None, None),
    )
    out_specs = (
        P("gx", "gy", None, None, None, None),
        P("gx", "gy", None, None, None),
        P("gx", "gy", None, None, None),
    )
    return jax.shard_map(
        per_device, mesh=mesh, in_specs=in_specs, out_specs=out_specs, check_vma=False
    )
```

```python
import functools

import jax
import jax.numpy as jnp
from jax import lax
from jax.experimental import pallas as pl
from jax.experimental.pallas import tpu as pltpu
from jax.sharding import PartitionSpec as P

MESH = pl.DeviceIdType.MESH
F32 = jnp.float32

STEPS = 2
TILES = 8
CELLS = 1024
LANES = 128
CHUNKS = CELLS // LANES
BASE = 32
EXTRA = 224
GROUP = 32
HALF = 16

time_step = 0.05
weissenberg = 0.25
max_extension = 50.0
noise_scale = (time_step / weissenberg) ** 0.5
relax_scale = time_step * (0.5 / weissenberg)
component_pairs = ((0, 0), (1, 1), (2, 2), (0, 1), (0, 2), (1, 2))
early_pairs = [(i, j) for j in range(6) for i in range(j + 1)]
late_pairs = [(i, j) for j in range(6, 9) for i in range(j + 1)]
moment_at = {pair: n for n, pair in enumerate(early_pairs + late_pairs)}


def wide(row):
    return jnp.broadcast_to(row, (GROUP, LANES))


def matrix(grad_row, keep_row):
    keep = wide(keep_row)
    rows = []
    for a in range(3):
        row = [wide(grad_row(3 * a + b)) for b in range(3)]
        row[a] = row[a] + keep
        rows.append(row)
    return rows


def advance(mat, state, noise):
    return [
        mat[a][0] * state[0]
        + mat[a][1] * state[1]
        + mat[a][2] * state[2]
        + noise_scale * noise[a].astype(F32)
        for a in range(3)
    ]


def fold(block):
    out = block[:8]
    for k in range(1, block.shape[0] // 8):
        out = out + block[8 * k : 8 * k + 8]
    return out


def inner(left, right):
    return fold(left[0] * right[0] + left[1] * right[1] + left[2] * right[2])


def products(state):
    return [fold(state[a] * state[b]) for a, b in component_pairs]


def row_sum(block):
    return jnp.sum(block, axis=0, keepdims=True)


def relaxation(total, count):
    return relax_scale * (1.0 / (1.0 - total / count / max_extension))


def helper_slots(helper, gy, n_gy, t):
    slot, hit = jnp.int32(0), jnp.int32(0)
    for h in range(n_gy):
        match = helper[h] == gy * TILES + t
        slot = jnp.where(match, lax.rem(gy - h + n_gy, n_gy), slot)
        hit = jnp.where(match, 1, hit)
    return slot, hit


def swap_blocks(regs, block):
    for bit in (1, 2, 4):
        upper = (block & bit) != 0
        new = list(regs)
        for i in range(8):
            if i & bit:
                continue
            j = i | bit
            new[i] = jnp.where(upper, pltpu.roll(regs[j], 16 * bit, 1), regs[i])
            new[j] = jnp.where(upper, regs[j], pltpu.roll(regs[i], LANES - 16 * bit, 1))
        regs = new
    return regs


def gradient(velocity, z_edge, fluid, y_edge, x_edge, sub, lane):
    deep = lane % 16

    def turn(value, shift):
        shift = shift % LANES
        return pltpu.roll(value, shift, 1) if shift else value

    grads = []
    for a in range(3):
        v = velocity[a]
        low = jnp.broadcast_to(x_edge[a : a + 1], (8, LANES))
        high = jnp.broadcast_to(x_edge[3 + a : 4 + a], (8, LANES))
        before = jnp.where(sub == 0, low, pltpu.roll(v, 1, 0))
        after = jnp.where(sub == 7, high, pltpu.roll(v, 7, 0))
        grads.append((after - before) * fluid)
        before = jnp.where(lane < 16, turn(y_edge, -16 * a), turn(v, 16))
        after = jnp.where(lane >= 112, turn(y_edge, 16 * (4 - a)), turn(v, -16))
        grads.append((after - before) * fluid)
        before = jnp.where(deep == 0, turn(z_edge, -a), turn(v, 1))
        after = jnp.where(deep == 15, turn(z_edge, a), turn(v, -1))
        grads.append((after - before) * fluid)
    return grads


def exchange_kernel(
    n_gx,
    n_gy,
    counts_hbm,
    helper_hbm,
    vel_hbm,
    wall_hbm,
    base_hbm,
    extra_hbm,
    base_noise_hbm,
    extra_noise_hbm,
    base,
    drifted,
    extra,
    own_total,
    own_rows,
    moment_recv,
    counts,
    helper,
    vel,
    wall,
    base_noise,
    late_noise,
    extra_noise,
    y_send,
    x_halo,
    y_halo,
    second,
    flow_own,
    flow_send,
    flow_recv,
    sum_own,
    extra_sum,
    sum_send,
    sum_recv,
    edge_own,
    edge_send,
    edge_recv,
    extra_second,
    helper_map,
    tile_grad,
    relax,
    in_sem,
    tile_sem,
    halo_send_sem,
    halo_recv_sem,
    flow_send_sem,
    flow_recv_sem,
    sum_send_sem,
    sum_recv_sem,
    edge_send_sem,
    edge_recv_sem,
    moment_send_sem,
    moment_recv_sem,
):
    gx = lax.axis_index("gx")
    gy = lax.axis_index("gy")
    up_x, down_x = lax.rem(gx + 1, n_gx), lax.rem(gx + n_gx - 1, n_gx)
    up_y, down_y = lax.rem(gy + 1, n_gy), lax.rem(gy + n_gy - 1, n_gy)

    barrier = pltpu.get_barrier_semaphore()
    for k in range(1, n_gy):
        peer = lax.rem(gy + k, n_gy)
        pl.semaphore_signal(barrier, inc=1, device_id=(gx, peer), device_id_type=MESH)
    for peer in (up_x, down_x):
        pl.semaphore_signal(barrier, inc=1, device_id=(peer, gy), device_id_type=MESH)

    vel_copy = pltpu.make_async_copy(vel_hbm, vel, in_sem.at[0])
    wall_copy = pltpu.make_async_copy(wall_hbm, wall, in_sem.at[1])
    helper_copy = pltpu.make_async_copy(helper_hbm, helper, in_sem.at[7])
    counts_copy = pltpu.make_async_copy(counts_hbm, counts, in_sem.at[8])
    extra_copy = pltpu.make_async_copy(extra_hbm, extra, in_sem.at[2])
    base_copies = [
        pltpu.make_async_copy(base_hbm.at[t], base.at[t], tile_sem.at[t]) for t in range(TILES)
    ]
    base_noise_copies = [
        pltpu.make_async_copy(base_noise_hbm.at[:, 0], base_noise, in_sem.at[3]),
        pltpu.make_async_copy(base_noise_hbm.at[:, 1], late_noise, in_sem.at[4]),
    ]
    extra_noise_copies = [
        pltpu.make_async_copy(extra_noise_hbm.at[s], extra_noise.at[s], in_sem.at[5 + s])
        for s in range(STEPS)
    ]
    vel_copy.start()
    wall_copy.start()
    helper_copy.start()
    counts_copy.start()
    for copy in base_copies:
        copy.start()
    base_noise_copies[0].start()
    extra_copy.start()
    extra_noise_copies[0].start()
    extra_noise_copies[1].start()
    base_noise_copies[1].start()

    def send_all(src_of, dst_of, send_sem, recv_sem):
        copies = [
            pltpu.make_async_remote_copy(
                src_ref=src_of(k),
                dst_ref=dst_of(k),
                send_sem=send_sem(k),
                recv_sem=recv_sem(k),
                device_id=(gx, lax.rem(gy + k, n_gy)),
                device_id_type=MESH,
            )
            for k in range(1, n_gy)
        ]
        for copy in copies:
            copy.start()
        return copies

    def wanted(k):
        return lax.rem(helper[lax.rem(gy + k, n_gy)], TILES)

    sub = lax.broadcasted_iota(jnp.int32, (8, LANES), 0)
    lane = lax.broadcasted_iota(jnp.int32, (8, LANES), 1)
    block = lane // 16
    deep = lane % 16
    vel_copy.wait()
    for c in range(3):
        y_send[0, c] = vel[c, :, 7, :]
        y_send[1, c] = vel[c, :, 0, :]
    x_halo[6:] = jnp.zeros((2, 8, LANES), F32)
    flow = [swap_blocks([vel[a, :, y, :] for y in range(8)], block) for a in range(3)]
    for t in range(TILES):
        z_edge = jnp.zeros((8, LANES), F32)
        for a in range(3):
            if t > 0:
                z_edge = jnp.where(deep == a, pltpu.roll(flow[a][t - 1], 113 + a, 1), z_edge)
            if t < TILES - 1:
                z_edge = jnp.where(deep == 15 - a, pltpu.roll(flow[a][t + 1], 15 - a, 1), z_edge)
            flow_own[t, a] = flow[a][t]
        flow_own[t, 3] = z_edge
    wall_copy.wait()
    fluid = swap_blocks(
        [jnp.where(wall[:, y, :] == 0, 0.5 * time_step, 0.0).astype(F32) for y in range(8)], block
    )
    for t in range(TILES):
        flow_own[t, 4] = fluid[t]
    helper_copy.wait()
    counts_copy.wait()

    @pl.loop(0, n_gy)
    def _(k):
        flow_send[k] = flow_own[wanted(k)]

    pl.semaphore_wait(barrier, n_gy + 1)

    halo_copies = [
        pltpu.make_async_remote_copy(
            src_ref=src,
            dst_ref=dst,
            send_sem=halo_send_sem.at[i],
            recv_sem=halo_recv_sem.at[i],
            device_id=device,
            device_id_type=MESH,
        )
        for i, (src, dst, device) in enumerate(
            (
                (vel.at[:, 7], x_halo.at[0:3], (up_x, gy)),
                (vel.at[:, 0], x_halo.at[3:6], (down_x, gy)),
                (y_send.at[0], y_halo.at[0:3], (gx, up_y)),
                (y_send.at[1], y_halo.at[3:6], (gx, down_y)),
            )
        )
    ]
    for copy in halo_copies:
        copy.start()
    flow_copies = send_all(
        lambda k: flow_send.at[k],
        lambda k: flow_recv.at[k],
        lambda k: flow_send_sem.at[k],
        lambda k: flow_recv_sem.at[k],
    )
    flow_recv[0] = flow_send[0]

    my_slot = lax.rem(gy - helper[gy] // TILES + n_gy, n_gy)
    slots = [helper_slots(helper, gy, n_gy, t) for t in range(TILES)]

    for copy in base_copies:
        copy.wait()
    base_noise_copies[0].wait()

    @pl.loop(0, TILES)
    def _(t):
        for x in range(CHUNKS):
            lanes = pl.ds(x * LANES, LANES)
            state = [base[t, c, :, lanes] for c in range(3)]
            noise = [base_noise[t, c, :, lanes].astype(F32) for c in range(3)]
            for m, total in enumerate(products(state)):
                second[t, m, pl.ds(x, 1), :] = row_sum(total)
            for a in range(3):
                for b in range(3):
                    second[t, 6 + 3 * a + b, pl.ds(x, 1), :] = row_sum(fold(state[a] * noise[b]))
            second[t, 15, pl.ds(x, 1), :] = row_sum(inner(noise, noise))

    for t in range(TILES):
        sum_own[t] = second[t, 0] + second[t, 1] + second[t, 2]

    extra_copy.wait()

    @pl.loop(0, CHUNKS)
    def _(x):
        lanes = pl.ds(pl.multiple_of(x * LANES, LANES), LANES)
        total = jnp.zeros((8, LANES), F32)
        for f in range(EXTRA // GROUP):
            state = [extra[c, pl.ds(f * GROUP, GROUP), lanes] for c in range(3)]
            total = total + inner(state, state)
        extra_sum[pl.ds(x, 1), :] = row_sum(total)

    @pl.loop(0, n_gy)
    def _(k):
        sum_send[k, 0] = sum_own[wanted(k)]
        sum_send[k, 1] = extra_sum[...]

    sum_copies = send_all(
        lambda k: sum_send.at[k],
        lambda k: sum_recv.at[k],
        lambda k: sum_send_sem.at[k],
        lambda k: sum_recv_sem.at[k],
    )
    sum_recv[0] = sum_send[0]

    for copy in halo_copies:
        copy.wait_recv()
    low = jnp.where(gx > 0, 1.0, 0.0)
    high = jnp.where(gx < n_gx - 1, 1.0, 0.0)
    inside = jnp.where(sub < 3, low, high)
    x_edges = swap_blocks([x_halo[:, y, :] * inside for y in range(8)], block)
    sides = [jnp.where(gy > 0, y_halo[a], 0.0) for a in range(3)]
    sides += [jnp.where(gy < n_gy - 1, y_halo[3 + a], 0.0) for a in range(3)]
    sides += [jnp.zeros((8, LANES), F32)] * 2
    y_edges = swap_blocks(sides, block)
    for t in range(TILES):
        edge_own[t, 0] = y_edges[t]
        edge_own[t, 1] = x_edges[t]

    @pl.loop(0, TILES)
    def _(t):
        grads = gradient(
            [flow_own[t, a] for a in range(3)],
            flow_own[t, 3],
            flow_own[t, 4],
            edge_own[t, 0],
            edge_own[t, 1],
            sub,
            lane,
        )
        for c in range(9):
            tile_grad[t, c] = grads[c]
        mat = [[grads[3 * a + b] + (1.0 if a == b else 0.0) for b in range(3)] for a in range(3)]
        pairs = {}
        for m, (a, b) in enumerate(component_pairs):
            pairs[a, b] = pairs[b, a] = second[t, m]
        cross = [[second[t, 6 + 3 * a + b] for b in range(3)] for a in range(3)]
        once = noise_scale * (cross[0][0] + cross[1][1] + cross[2][2])
        twice = (noise_scale * noise_scale) * second[t, 15]
        for a in range(3):
            for b in range(3):
                inner_row = (
                    mat[a][0] * pairs[0, b] + mat[a][1] * pairs[1, b] + mat[a][2] * pairs[2, b]
                )
                once = once + (mat[a][b] * pairs[a, b])
                twice = twice + mat[a][b] * (inner_row + (2.0 * noise_scale) * cross[b][a])
        edge_own[t, 2] = once
        edge_own[t, 3] = twice

    @pl.loop(0, n_gy)
    def _(k):
        edge_send[k] = edge_own[wanted(k)]

    edge_copies = send_all(
        lambda k: edge_send.at[k],
        lambda k: edge_recv.at[k],
        lambda k: edge_send_sem.at[k],
        lambda k: edge_recv_sem.at[k],
    )
    edge_recv[0] = edge_send[0]

    for copy in extra_noise_copies:
        copy.wait()
    for wanted_pairs in (early_pairs, late_pairs):

        @pl.loop(0, CHUNKS)
        def _(x):
            lanes = pl.ds(pl.multiple_of(x * LANES, LANES), LANES)
            totals = [jnp.zeros((8, LANES), F32) for _ in wanted_pairs]
            for f in range(EXTRA // HALF):
                fields = pl.ds(f * HALF, HALF)
                parts = [extra[c, fields, lanes] for c in range(3)]
                for s in range(STEPS):
                    parts += [extra_noise[s, c, fields, lanes].astype(F32) for c in range(3)]
                totals = [
                    total + fold(parts[i] * parts[j])
                    for total, (i, j) in zip(totals, wanted_pairs)
                ]
            for pair, total in zip(wanted_pairs, totals):
                extra_second[moment_at[pair], pl.ds(x, 1), :] = row_sum(total)

    for copy in sum_copies:
        copy.wait_recv()
    for t in range(TILES):
        slot, hit = slots[t]
        count = jnp.full((CHUNKS, LANES), counts[t], jnp.int32).astype(F32)
        total = sum_own[t] + jnp.where(hit == 1, sum_recv[slot, 1], 0.0)
        rate = relaxation(total, count)
        relax[t] = 1.0 - rate
        own_total[t] = edge_own[t, 3] - rate * (2.0 * edge_own[t, 2] - rate * sum_own[t])

    @pl.loop(0, TILES)
    def _(t):
        for x in range(CHUNKS):
            lanes = pl.ds(x * LANES, LANES)
            mat = matrix(lambda c: tile_grad[t, c, pl.ds(x, 1), :], relax[t, pl.ds(x, 1), :])
            state = [base[t, c, :, lanes] for c in range(3)]
            state = advance(mat, state, [base_noise[t, c, :, lanes] for c in range(3)])
            for c in range(3):
                base[t, c, :, lanes] = state[c]

    for copies in (flow_copies, edge_copies):
        for copy in copies:
            copy.wait_recv()
    grads = gradient(
        [flow_recv[my_slot, a] for a in range(3)],
        flow_recv[my_slot, 3],
        flow_recv[my_slot, 4],
        edge_recv[my_slot, 0],
        edge_recv[my_slot, 1],
        sub,
        lane,
    )
    first = sum_recv[my_slot, 0]
    rate = relaxation(first + extra_sum[...], 256.0)
    own_share = edge_recv[my_slot, 3] - rate * (2.0 * edge_recv[my_slot, 2] - rate * first)

    def pair_sum(i, j):
        return extra_second[moment_at[min(i, j), max(i, j)]]

    def step_matrix(keep):
        return [
            [grads[3 * a + b] + keep if a == b else grads[3 * a + b] for b in range(3)]
            for a in range(3)
        ]

    def dot(left, right):
        out = left[0] * right[0]
        for u, v in zip(left[1:], right[1:]):
            out = out + u * v
        return out

    one = step_matrix(1.0 - rate)
    total = jnp.zeros((8, LANES), F32)
    for a in range(3):
        mixed = [
            dot(one[a], [pair_sum(i, j) for i in range(3)]) + noise_scale * pair_sum(3 + a, j)
            for j in (0, 1, 2, 3 + a)
        ]
        total = total + dot(one[a], mixed[:3]) + noise_scale * mixed[3]
    moment_recv[0, 6] = total
    two = step_matrix(1.0 - relaxation(total + own_share, 256.0))
    combined = []
    for a in range(3):
        row = [dot(two[a], [one[c][b] for c in range(3)]) for b in range(3)]
        row += [noise_scale * two[a][b] for b in range(3)]
        combined.append(row)
        for b in range(6):
            helper_map[6 * a + b] = row[b]
    for a in range(3):
        mixed = [
            dot(combined[a], [pair_sum(i, j) for i in range(6)]) + noise_scale * pair_sum(6 + a, j)
            for j in range(9)
        ]
        for m, (first_axis, second_axis) in enumerate(component_pairs):
            if first_axis == a:
                moment_recv[0, m] = (
                    dot(combined[second_axis], mixed[:6]) + noise_scale * mixed[6 + second_axis]
                )

    moment_copies = send_all(
        lambda k: moment_recv.at[0],
        lambda k: moment_recv.at[k],
        lambda k: moment_send_sem.at[k],
        lambda k: moment_recv_sem.at[k],
    )

    @pl.loop(0, CHUNKS)
    def _(x):
        lanes = pl.ds(pl.multiple_of(x * LANES, LANES), LANES)
        rows = [
            jnp.broadcast_to(helper_map[n, pl.ds(x, 1), :], (HALF, LANES)) for n in range(18)
        ]
        for f in range(EXTRA // HALF):
            fields = pl.ds(f * HALF, HALF)
            parts = [extra[c, fields, lanes] for c in range(3)]
            parts += [extra_noise[0, c, fields, lanes].astype(F32) for c in range(3)]
            for a in range(3):
                last = extra_noise[1, a, fields, lanes].astype(F32)
                extra[a, fields, lanes] = dot(rows[6 * a : 6 * a + 6], parts) + noise_scale * last

    base_noise_copies[1].wait()

    @pl.loop(0, TILES)
    def _(t):
        for x in range(CHUNKS):
            lanes = pl.ds(x * LANES, LANES)
            mat = matrix(lambda c: tile_grad[t, c, pl.ds(x, 1), :], jnp.ones((1, LANES), F32))
            state = [base[t, c, :, lanes] for c in range(3)]
            moved = advance(mat, state, [late_noise[t, c, :, lanes] for c in range(3)])
            for c in range(3):
                drifted[t, c, :, lanes] = moved[c]
            for m, (a, b) in enumerate(component_pairs):
                here = pl.ds(x, 1)
                own_rows[t, m, here, :] = row_sum(fold(moved[a] * moved[b]))
                if a == b:
                    own_rows[t, 6 + m, here, :] = 2.0 * row_sum(fold(moved[a] * state[a]))
                else:
                    both = fold(moved[a] * state[b] + moved[b] * state[a])
                    own_rows[t, 6 + m, here, :] = row_sum(both)
                own_rows[t, 12 + m, here, :] = row_sum(fold(state[a] * state[b]))

    for copies in (halo_copies, flow_copies, sum_copies, edge_copies):
        for copy in copies:
            copy.wait_send()
    for copy in moment_copies:
        copy.wait_recv()
        copy.wait_send()


def finish_kernel(
    n_gy,
    counts_hbm,
    helper_hbm,
    start,
    drifted,
    extra,
    own_total,
    own_rows,
    moment_recv,
    base_out,
    extra_out,
    stress_out,
    counts,
    helper,
    base,
    stress,
    staged,
    relax,
    tile_sem,
    out_sem,
):
    gy = lax.axis_index("gy")
    helper_copy = pltpu.make_async_copy(helper_hbm, helper, out_sem.at[2])
    counts_copy = pltpu.make_async_copy(counts_hbm, counts, out_sem.at[3])
    extra_copy = pltpu.make_async_copy(extra, extra_out, out_sem.at[0])
    helper_copy.start()
    counts_copy.start()
    extra_copy.start()
    helper_copy.wait()
    counts_copy.wait()
    slots = [helper_slots(helper, gy, n_gy, t) for t in range(TILES)]
    tile_counts = [jnp.full((CHUNKS, LANES), counts[t], jnp.int32).astype(F32) for t in range(TILES)]
    for t in range(TILES):
        slot, hit = slots[t]
        total = own_total[t] + jnp.where(hit == 1, moment_recv[slot, 6], 0.0)
        relax[t] = relaxation(total, tile_counts[t])

    @pl.loop(0, TILES)
    def _(t):
        for x in range(CHUNKS):
            lanes = pl.ds(x * LANES, LANES)
            rate = wide(relax[t, pl.ds(x, 1), :])
            for c in range(3):
                base[t, c, :, lanes] = drifted[t, c, :, lanes] - rate * start[t, c, :, lanes]
        pltpu.make_async_copy(base.at[t], base_out.at[t], tile_sem.at[t]).start()

    for t in range(TILES):
        slot, hit = slots[t]
        rate = relax[t]
        second = []
        for m in range(6):
            own = own_rows[t, m] - rate * (own_rows[t, 6 + m] - rate * own_rows[t, 12 + m])
            second.append((own + jnp.where(hit == 1, moment_recv[slot, m], 0.0)) / tile_counts[t])
        trace = second[0] + second[1] + second[2]
        stretch = 1.0 / (1.0 - trace / max_extension)
        for m in range(6):
            staged[m, :, t, :] = (stretch * second[m] - (1.0 if m < 3 else 0.0)) / weissenberg

    for m in range(6):
        for x in range(CHUNKS):
            stress[m, :, pl.ds(x * LANES, LANES)] = staged[m, x]

    stress_copy = pltpu.make_async_copy(stress, stress_out, out_sem.at[1])
    stress_copy.start()
    for t in range(TILES):
        pltpu.make_async_copy(base.at[t], base_out.at[t], tile_sem.at[t]).wait()
    extra_copy.wait()
    stress_copy.wait()


def hold(array):
    return pltpu.with_memory_space_constraint(array, pltpu.HBM)


def solution(mesh):
    n_gx, n_gy = mesh.shape["gx"], mesh.shape["gy"]

    def per_device(
        velocity,
        wall_cells,
        tile_counts,
        helper_tile,
        base_fields,
        extra_fields,
        base_noise,
        extra_noise,
    ):
        hbm = pl.BlockSpec(memory_space=pltpu.HBM)
        vmem = pl.BlockSpec(memory_space=pltpu.VMEM)
        dma = pltpu.SemaphoreType.DMA
        counts = hold(tile_counts.reshape(TILES))
        helper = hold(helper_tile.reshape(n_gy))

        def block(*lead):
            return pltpu.VMEM((*lead, CHUNKS, LANES), F32)

        passed = pl.pallas_call(
            functools.partial(exchange_kernel, n_gx, n_gy),
            out_shape=(
                jax.ShapeDtypeStruct((TILES, 3, BASE, CELLS), F32),
                jax.ShapeDtypeStruct((TILES, 3, BASE, CELLS), F32),
                jax.ShapeDtypeStruct((3, EXTRA, CELLS), F32),
                jax.ShapeDtypeStruct((TILES, CHUNKS, LANES), F32),
                jax.ShapeDtypeStruct((TILES, 18, CHUNKS, LANES), F32),
                jax.ShapeDtypeStruct((n_gy, 7, CHUNKS, LANES), F32),
            ),
            in_specs=[hbm] * 8,
            out_specs=(vmem,) * 6,
            scratch_shapes=[
                pltpu.SMEM((TILES,), jnp.int32),
                pltpu.SMEM((n_gy,), jnp.int32),
                block(3, 8),
                pltpu.VMEM((8, 8, LANES), jnp.int32),
                pltpu.VMEM((TILES, 3, BASE, CELLS), jnp.bfloat16),
                pltpu.VMEM((TILES, 3, BASE, CELLS), jnp.bfloat16),
                pltpu.VMEM((STEPS, 3, EXTRA, CELLS), jnp.bfloat16),
                block(2, 3),
                block(8),
                block(6),
                block(TILES, 16),
                block(TILES, 5),
                block(n_gy, 5),
                block(n_gy, 5),
                block(TILES),
                block(),
                block(n_gy, 2),
                block(n_gy, 2),
                block(TILES, 4),
                block(n_gy, 4),
                block(n_gy, 4),
                block(45),
                block(18),
                block(TILES, 9),
                block(TILES),
                dma((9,)),
                dma((TILES,)),
                dma((4,)),
                dma((4,)),
                dma((n_gy,)),
                dma((n_gy,)),
                dma((n_gy,)),
                dma((n_gy,)),
                dma((n_gy,)),
                dma((n_gy,)),
                dma((n_gy,)),
                dma((n_gy,)),
            ],
            compiler_params=pltpu.CompilerParams(
                collective_id=0, has_side_effects=True, vmem_limit_bytes=40 << 20
            ),
        )(
            counts,
            helper,
            hold(velocity),
            hold(wall_cells),
            hold(base_fields.reshape(TILES, 3, BASE, CELLS)),
            hold(extra_fields.reshape(3, EXTRA, CELLS)),
            hold(base_noise.reshape(TILES, STEPS, 3, BASE, CELLS)),
            hold(extra_noise.reshape(STEPS, 3, EXTRA, CELLS)),
        )
        base_out, extra_out, stress_out = pl.pallas_call(
            functools.partial(finish_kernel, n_gy),
            out_shape=(
                jax.ShapeDtypeStruct((TILES, 3, BASE, CELLS), F32),
                jax.ShapeDtypeStruct((3, EXTRA, CELLS), F32),
                jax.ShapeDtypeStruct((6, TILES, CELLS), F32),
            ),
            in_specs=[hbm] * 2 + [vmem] * 6,
            out_specs=(hbm,) * 3,
            scratch_shapes=[
                pltpu.SMEM((TILES,), jnp.int32),
                pltpu.SMEM((n_gy,), jnp.int32),
                pltpu.VMEM((TILES, 3, BASE, CELLS), F32),
                pltpu.VMEM((6, TILES, CELLS), F32),
                pltpu.VMEM((6, CHUNKS, TILES, LANES), F32),
                block(TILES),
                dma((TILES,)),
                dma((4,)),
            ],
            compiler_params=pltpu.CompilerParams(vmem_limit_bytes=40 << 20),
        )(counts, helper, *passed)
        return base_out[None, None], extra_out[None, None], stress_out.transpose(1, 0, 2)[None, None]

    in_specs = (
        P(None, "gx", "gy", None),
        P("gx", "gy", None),
        P("gx", "gy", None),
        P("gx", None),
        P("gx", "gy", None, None, None, None),
        P("gx", "gy", None, None, None),
        P("gx", "gy", None, None, None, None, None),
        P("gx", "gy", None, None, None, None),
    )
    out_specs = (
        P("gx", "gy", None, None, None, None),
        P("gx", "gy", None, None, None),
        P("gx", "gy", None, None, None),
    )
    return jax.shard_map(
        per_device, mesh=mesh, in_specs=in_specs, out_specs=out_specs, check_vma=False
    )
```

```python
import functools

import jax
import jax.numpy as jnp
from jax import lax
from jax.experimental import pallas as pl
from jax.experimental.pallas import tpu as pltpu
from jax.sharding import PartitionSpec as P

MESH = pl.DeviceIdType.MESH
F32 = jnp.float32

STEPS = 2
TILES = 8
CELLS = 1024
LANES = 128
CHUNKS = CELLS // LANES
BASE = 32
EXTRA = 224
GROUP = 32
HALF = 16

time_step = 0.05
weissenberg = 0.25
max_extension = 50.0
noise_scale = (time_step / weissenberg) ** 0.5
relax_scale = time_step * (0.5 / weissenberg)
component_pairs = ((0, 0), (1, 1), (2, 2), (0, 1), (0, 2), (1, 2))
early_pairs = [(i, j) for j in range(6) for i in range(j + 1)]
late_pairs = [(i, j) for j in range(6, 9) for i in range(j + 1)]
moment_at = {pair: n for n, pair in enumerate(early_pairs + late_pairs)}


def wide(row):
    return jnp.broadcast_to(row, (GROUP, LANES))


def matrix(grad_row, keep_row):
    keep = wide(keep_row)
    rows = []
    for a in range(3):
        row = [wide(grad_row(3 * a + b)) for b in range(3)]
        row[a] = row[a] + keep
        rows.append(row)
    return rows


def advance(mat, state, noise):
    return [
        mat[a][0] * state[0]
        + mat[a][1] * state[1]
        + mat[a][2] * state[2]
        + noise_scale * noise[a].astype(F32)
        for a in range(3)
    ]


def fold(block):
    out = block[:8]
    for k in range(1, block.shape[0] // 8):
        out = out + block[8 * k : 8 * k + 8]
    return out


def inner(left, right):
    return fold(left[0] * right[0] + left[1] * right[1] + left[2] * right[2])


def products(state):
    return [fold(state[a] * state[b]) for a, b in component_pairs]


def row_sum(block):
    return jnp.sum(block, axis=0, keepdims=True)


def relaxation(total, count):
    return relax_scale * (1.0 / (1.0 - total / count / max_extension))


SIDE = 4
offsets = sorted(
    range(1, SIDE * SIDE), key=lambda k: -sum(min(v, SIDE - v) for v in divmod(k, SIDE))
)


def wrap(value):
    return lax.rem(value + SIDE, SIDE)


def shifted(gy, k):
    x, y = gy // SIDE, lax.rem(gy, SIDE)
    return wrap(x + k // SIDE) * SIDE + wrap(y + k % SIDE)


def slot_from(gy, sender):
    x, y = gy // SIDE, lax.rem(gy, SIDE)
    return wrap(x - sender // SIDE) * SIDE + wrap(y - lax.rem(sender, SIDE))


def helper_slots(helper, gy, n_gy, t):
    slot, hit = jnp.int32(0), jnp.int32(0)
    for h in range(n_gy):
        match = helper[h] == gy * TILES + t
        slot = jnp.where(match, slot_from(gy, h), slot)
        hit = jnp.where(match, 1, hit)
    return slot, hit


def swap_blocks(regs, block):
    for bit in (1, 2, 4):
        upper = (block & bit) != 0
        new = list(regs)
        for i in range(8):
            if i & bit:
                continue
            j = i | bit
            new[i] = jnp.where(upper, pltpu.roll(regs[j], 16 * bit, 1), regs[i])
            new[j] = jnp.where(upper, regs[j], pltpu.roll(regs[i], LANES - 16 * bit, 1))
        regs = new
    return regs


def gradient(velocity, z_edge, fluid, y_edge, x_edge, sub, lane):
    deep = lane % 16

    def turn(value, shift):
        shift = shift % LANES
        return pltpu.roll(value, shift, 1) if shift else value

    grads = []
    for a in range(3):
        v = velocity[a]
        low = jnp.broadcast_to(x_edge[a : a + 1], (8, LANES))
        high = jnp.broadcast_to(x_edge[3 + a : 4 + a], (8, LANES))
        before = jnp.where(sub == 0, low, pltpu.roll(v, 1, 0))
        after = jnp.where(sub == 7, high, pltpu.roll(v, 7, 0))
        grads.append((after - before) * fluid)
        before = jnp.where(lane < 16, turn(y_edge, -16 * a), turn(v, 16))
        after = jnp.where(lane >= 112, turn(y_edge, 16 * (4 - a)), turn(v, -16))
        grads.append((after - before) * fluid)
        before = jnp.where(deep == 0, turn(z_edge, -a), turn(v, 1))
        after = jnp.where(deep == 15, turn(z_edge, a), turn(v, -1))
        grads.append((after - before) * fluid)
    return grads


def exchange_kernel(
    n_gx,
    n_gy,
    counts_hbm,
    helper_hbm,
    vel_hbm,
    wall_hbm,
    base_hbm,
    extra_hbm,
    base_noise_hbm,
    extra_noise_hbm,
    base,
    drifted,
    extra,
    own_total,
    own_rows,
    moment_recv,
    counts,
    helper,
    vel,
    wall,
    base_noise,
    late_noise,
    extra_noise,
    y_send,
    x_halo,
    y_halo,
    second,
    layer_own,
    flow_own,
    flow_send,
    flow_recv,
    sum_own,
    extra_sum,
    sum_send,
    sum_recv,
    edge_own,
    edge_send,
    edge_recv,
    extra_second,
    helper_map,
    tile_grad,
    relax,
    in_sem,
    tile_sem,
    halo_send_sem,
    halo_recv_sem,
    flow_send_sem,
    flow_recv_sem,
    sum_send_sem,
    sum_recv_sem,
    edge_send_sem,
    edge_recv_sem,
    moment_send_sem,
    moment_recv_sem,
    ring_sem,
):
    gx = lax.axis_index("gx")
    gy = lax.axis_index("gy")
    up_x, down_x = lax.rem(gx + 1, n_gx), lax.rem(gx + n_gx - 1, n_gx)
    up_y, down_y = lax.rem(gy + 1, n_gy), lax.rem(gy + n_gy - 1, n_gy)

    barrier = pltpu.get_barrier_semaphore()
    near = [(gx, up_y), (gx, down_y), (up_x, gy), (down_x, gy)]
    near += [(gx, shifted(gy, v)) for v in range(1, SIDE)]
    near += [(gx, shifted(gy, v * SIDE)) for v in range(1, SIDE)]
    for device in near:
        pl.semaphore_signal(barrier, inc=1, device_id=device, device_id_type=MESH)

    vel_copy = pltpu.make_async_copy(vel_hbm, vel, in_sem.at[0])
    wall_copy = pltpu.make_async_copy(wall_hbm, wall, in_sem.at[1])
    helper_copy = pltpu.make_async_copy(helper_hbm, helper, in_sem.at[7])
    counts_copy = pltpu.make_async_copy(counts_hbm, counts, in_sem.at[8])
    extra_copy = pltpu.make_async_copy(extra_hbm, extra, in_sem.at[2])
    base_copies = [
        pltpu.make_async_copy(base_hbm.at[t], base.at[t], tile_sem.at[t]) for t in range(TILES)
    ]
    base_noise_copies = [
        pltpu.make_async_copy(base_noise_hbm.at[:, 0], base_noise, in_sem.at[3]),
        pltpu.make_async_copy(base_noise_hbm.at[:, 1], late_noise, in_sem.at[4]),
    ]
    extra_noise_copies = [
        pltpu.make_async_copy(extra_noise_hbm.at[s], extra_noise.at[s], in_sem.at[5 + s])
        for s in range(STEPS)
    ]
    vel_copy.start()
    wall_copy.start()
    helper_copy.start()
    counts_copy.start()
    for copy in base_copies:
        copy.start()
    base_noise_copies[0].start()
    extra_copy.start()
    extra_noise_copies[0].start()
    extra_noise_copies[1].start()
    base_noise_copies[1].start()

    def send_all(src_of, dst_of, send_sem, recv_sem):
        copies = [
            pltpu.make_async_remote_copy(
                src_ref=src_of(k),
                dst_ref=dst_of(k),
                send_sem=send_sem(k),
                recv_sem=recv_sem(k),
                device_id=(gx, shifted(gy, k)),
                device_id_type=MESH,
            )
            for k in offsets
        ]
        for copy in copies:
            copy.start()
        return copies

    def wanted(k):
        return lax.rem(helper[shifted(gy, k)], TILES)

    sub = lax.broadcasted_iota(jnp.int32, (8, LANES), 0)
    lane = lax.broadcasted_iota(jnp.int32, (8, LANES), 1)
    block = lane // 16
    deep = lane % 16
    vel_copy.wait()
    for c in range(3):
        y_send[0, c] = vel[c, :, 7, :]
        y_send[1, c] = vel[c, :, 0, :]
    x_halo[6:] = jnp.zeros((2, 8, LANES), F32)
    flow = [swap_blocks([vel[a, :, y, :] for y in range(8)], block) for a in range(3)]
    for t in range(TILES):
        z_edge = jnp.zeros((8, LANES), F32)
        for a in range(3):
            if t > 0:
                z_edge = jnp.where(deep == a, pltpu.roll(flow[a][t - 1], 113 + a, 1), z_edge)
            if t < TILES - 1:
                z_edge = jnp.where(deep == 15 - a, pltpu.roll(flow[a][t + 1], 15 - a, 1), z_edge)
            flow_own[t, a] = flow[a][t]
        flow_own[t, 3] = z_edge
    wall_copy.wait()
    fluid = swap_blocks(
        [jnp.where(wall[:, y, :] == 0, 0.5 * time_step, 0.0).astype(F32) for y in range(8)], block
    )
    for t in range(TILES):
        flow_own[t, 4] = fluid[t]
    sides = [y_send[0, a] for a in range(3)] + [y_send[1, a] for a in range(3)]
    layers = swap_blocks(sides + [jnp.zeros((8, LANES), F32)] * 2, block)
    for t in range(TILES):
        layer_own[t] = layers[t]
    helper_copy.wait()
    counts_copy.wait()

    @pl.loop(0, n_gy)
    def _(k):
        tile = wanted(k)
        flow_send[k] = flow_own[tile]
        mine = helper[shifted(gy, k)] // TILES == gy
        flow_send[k, 0] = jnp.where(mine, flow_own[tile, 0], layer_own[tile])

    pl.semaphore_wait(barrier, len(near))

    halo_copies = [
        pltpu.make_async_remote_copy(
            src_ref=src,
            dst_ref=dst,
            send_sem=halo_send_sem.at[i],
            recv_sem=halo_recv_sem.at[i],
            device_id=device,
            device_id_type=MESH,
        )
        for i, (src, dst, device) in enumerate(
            (
                (vel.at[:, 7], x_halo.at[0:3], (up_x, gy)),
                (vel.at[:, 0], x_halo.at[3:6], (down_x, gy)),
                (y_send.at[0], y_halo.at[0:3], (gx, up_y)),
                (y_send.at[1], y_halo.at[3:6], (gx, down_y)),
            )
        )
    ]
    for copy in halo_copies:
        copy.start()
    for v in range(1, SIDE):
        pl.semaphore_signal(
            ring_sem, inc=1, device_id=(gx, shifted(gy, v)), device_id_type=MESH
        )
    pl.semaphore_wait(ring_sem, SIDE - 1)
    flow_copies = send_all(
        lambda k: flow_send.at[k],
        lambda k: flow_recv.at[k],
        lambda k: flow_send_sem.at[k],
        lambda k: flow_recv_sem.at[k],
    )
    flow_recv[0] = flow_send[0]

    owner = helper[gy] // TILES
    my_slot = slot_from(gy, owner)
    low_slot = slot_from(gy, lax.rem(owner + n_gy - 1, n_gy))
    high_slot = slot_from(gy, lax.rem(owner + 1, n_gy))
    slots = [helper_slots(helper, gy, n_gy, t) for t in range(TILES)]

    for copy in base_copies:
        copy.wait()
    base_noise_copies[0].wait()

    @pl.loop(0, TILES)
    def _(t):
        for x in range(CHUNKS):
            lanes = pl.ds(x * LANES, LANES)
            state = [base[t, c, :, lanes] for c in range(3)]
            noise = [base_noise[t, c, :, lanes].astype(F32) for c in range(3)]
            for m, total in enumerate(products(state)):
                second[t, m, pl.ds(x, 1), :] = row_sum(total)
            for a in range(3):
                for b in range(3):
                    second[t, 6 + 3 * a + b, pl.ds(x, 1), :] = row_sum(fold(state[a] * noise[b]))
            second[t, 15, pl.ds(x, 1), :] = row_sum(inner(noise, noise))

    for t in range(TILES):
        sum_own[t] = second[t, 0] + second[t, 1] + second[t, 2]

    extra_copy.wait()

    @pl.loop(0, CHUNKS)
    def _(x):
        lanes = pl.ds(pl.multiple_of(x * LANES, LANES), LANES)
        total = jnp.zeros((8, LANES), F32)
        for f in range(EXTRA // GROUP):
            state = [extra[c, pl.ds(f * GROUP, GROUP), lanes] for c in range(3)]
            total = total + inner(state, state)
        extra_sum[pl.ds(x, 1), :] = row_sum(total)

    @pl.loop(0, n_gy)
    def _(k):
        sum_send[k, 0] = sum_own[wanted(k)]
        sum_send[k, 1] = extra_sum[...]

    sum_copies = send_all(
        lambda k: sum_send.at[k],
        lambda k: sum_recv.at[k],
        lambda k: sum_send_sem.at[k],
        lambda k: sum_recv_sem.at[k],
    )
    sum_recv[0] = sum_send[0]

    for copy in halo_copies:
        copy.wait_recv()
    low = jnp.where(gx > 0, 1.0, 0.0)
    high = jnp.where(gx < n_gx - 1, 1.0, 0.0)
    inside = jnp.where(sub < 3, low, high)
    x_edges = swap_blocks([x_halo[:, y, :] * inside for y in range(8)], block)
    sides = [jnp.where(gy > 0, y_halo[a], 0.0) for a in range(3)]
    sides += [jnp.where(gy < n_gy - 1, y_halo[3 + a], 0.0) for a in range(3)]
    sides += [jnp.zeros((8, LANES), F32)] * 2
    y_edges = swap_blocks(sides, block)
    for t in range(TILES):
        layer_own[t] = y_edges[t]
        edge_own[t, 0] = x_edges[t]

    @pl.loop(0, TILES)
    def _(t):
        grads = gradient(
            [flow_own[t, a] for a in range(3)],
            flow_own[t, 3],
            flow_own[t, 4],
            layer_own[t],
            edge_own[t, 0],
            sub,
            lane,
        )
        for c in range(9):
            tile_grad[t, c] = grads[c]
        mat = [[grads[3 * a + b] + (1.0 if a == b else 0.0) for b in range(3)] for a in range(3)]
        pairs = {}
        for m, (a, b) in enumerate(component_pairs):
            pairs[a, b] = pairs[b, a] = second[t, m]
        cross = [[second[t, 6 + 3 * a + b] for b in range(3)] for a in range(3)]
        once = noise_scale * (cross[0][0] + cross[1][1] + cross[2][2])
        twice = (noise_scale * noise_scale) * second[t, 15]
        for a in range(3):
            for b in range(3):
                inner_row = (
                    mat[a][0] * pairs[0, b] + mat[a][1] * pairs[1, b] + mat[a][2] * pairs[2, b]
                )
                once = once + (mat[a][b] * pairs[a, b])
                twice = twice + mat[a][b] * (inner_row + (2.0 * noise_scale) * cross[b][a])
        edge_own[t, 1] = once
        edge_own[t, 2] = twice

    @pl.loop(0, n_gy)
    def _(k):
        edge_send[k] = edge_own[wanted(k)]

    edge_copies = send_all(
        lambda k: edge_send.at[k],
        lambda k: edge_recv.at[k],
        lambda k: edge_send_sem.at[k],
        lambda k: edge_recv_sem.at[k],
    )
    edge_recv[0] = edge_send[0]

    for copy in extra_noise_copies:
        copy.wait()
    for wanted_pairs in (early_pairs, late_pairs):

        @pl.loop(0, CHUNKS)
        def _(x):
            lanes = pl.ds(pl.multiple_of(x * LANES, LANES), LANES)
            totals = [jnp.zeros((8, LANES), F32) for _ in wanted_pairs]
            for f in range(EXTRA // HALF):
                fields = pl.ds(f * HALF, HALF)
                parts = [extra[c, fields, lanes] for c in range(3)]
                for s in range(STEPS):
                    parts += [extra_noise[s, c, fields, lanes].astype(F32) for c in range(3)]
                totals = [
                    total + fold(parts[i] * parts[j])
                    for total, (i, j) in zip(totals, wanted_pairs)
                ]
            for pair, total in zip(wanted_pairs, totals):
                extra_second[moment_at[pair], pl.ds(x, 1), :] = row_sum(total)

    for copies in (sum_copies, flow_copies, edge_copies):
        for copy in copies:
            copy.wait_recv()
    grads = gradient(
        [flow_recv[my_slot, a] for a in range(3)],
        flow_recv[my_slot, 3],
        flow_recv[my_slot, 4],
        jnp.where(
            block < 3,
            jnp.where(owner > 0, flow_recv[low_slot, 0], 0.0),
            jnp.where(owner < n_gy - 1, flow_recv[high_slot, 0], 0.0),
        ),
        edge_recv[my_slot, 0],
        sub,
        lane,
    )
    first = sum_recv[my_slot, 0]
    rate = relaxation(first + extra_sum[...], 256.0)
    own_share = edge_recv[my_slot, 2] - rate * (2.0 * edge_recv[my_slot, 1] - rate * first)

    def pair_sum(i, j):
        return extra_second[moment_at[min(i, j), max(i, j)]]

    def step_matrix(keep):
        return [
            [grads[3 * a + b] + keep if a == b else grads[3 * a + b] for b in range(3)]
            for a in range(3)
        ]

    def dot(left, right):
        out = left[0] * right[0]
        for u, v in zip(left[1:], right[1:]):
            out = out + u * v
        return out

    one = step_matrix(1.0 - rate)
    total = jnp.zeros((8, LANES), F32)
    for a in range(3):
        mixed = [
            dot(one[a], [pair_sum(i, j) for i in range(3)]) + noise_scale * pair_sum(3 + a, j)
            for j in (0, 1, 2, 3 + a)
        ]
        total = total + dot(one[a], mixed[:3]) + noise_scale * mixed[3]
    moment_recv[0, 6] = total
    two = step_matrix(1.0 - relaxation(total + own_share, 256.0))
    combined = []
    for a in range(3):
        row = [dot(two[a], [one[c][b] for c in range(3)]) for b in range(3)]
        row += [noise_scale * two[a][b] for b in range(3)]
        combined.append(row)
        for b in range(6):
            helper_map[6 * a + b] = row[b]
    for a in range(3):
        mixed = [
            dot(combined[a], [pair_sum(i, j) for i in range(6)]) + noise_scale * pair_sum(6 + a, j)
            for j in range(9)
        ]
        for m, (first_axis, second_axis) in enumerate(component_pairs):
            if first_axis == a:
                moment_recv[0, m] = (
                    dot(combined[second_axis], mixed[:6]) + noise_scale * mixed[6 + second_axis]
                )

    moment_copies = send_all(
        lambda k: moment_recv.at[0],
        lambda k: moment_recv.at[k],
        lambda k: moment_send_sem.at[k],
        lambda k: moment_recv_sem.at[k],
    )

    @pl.loop(0, CHUNKS)
    def _(x):
        lanes = pl.ds(pl.multiple_of(x * LANES, LANES), LANES)
        rows = [
            jnp.broadcast_to(helper_map[n, pl.ds(x, 1), :], (HALF, LANES)) for n in range(18)
        ]
        for f in range(EXTRA // HALF):
            fields = pl.ds(f * HALF, HALF)
            parts = [extra[c, fields, lanes] for c in range(3)]
            parts += [extra_noise[0, c, fields, lanes].astype(F32) for c in range(3)]
            for a in range(3):
                last = extra_noise[1, a, fields, lanes].astype(F32)
                extra[a, fields, lanes] = dot(rows[6 * a : 6 * a + 6], parts) + noise_scale * last

    for t in range(TILES):
        slot, hit = slots[t]
        count = jnp.full((CHUNKS, LANES), counts[t], jnp.int32).astype(F32)
        total = sum_own[t] + jnp.where(hit == 1, sum_recv[slot, 1], 0.0)
        rate = relaxation(total, count)
        relax[t] = rate
        own_total[t] = edge_own[t, 2] - rate * (2.0 * edge_own[t, 1] - rate * sum_own[t])

    base_noise_copies[1].wait()

    @pl.loop(0, TILES)
    def _(t):
        for x in range(CHUNKS):
            lanes = pl.ds(x * LANES, LANES)
            mat = matrix(lambda c: tile_grad[t, c, pl.ds(x, 1), :], jnp.ones((1, LANES), F32))
            rate = wide(relax[t, pl.ds(x, 1), :])
            start = [base[t, c, :, lanes] for c in range(3)]
            state = advance(mat, start, [base_noise[t, c, :, lanes] for c in range(3)])
            state = [state[c] - rate * start[c] for c in range(3)]
            for c in range(3):
                base[t, c, :, lanes] = state[c]
            moved = advance(mat, state, [late_noise[t, c, :, lanes] for c in range(3)])
            for c in range(3):
                drifted[t, c, :, lanes] = moved[c]
            for m, (a, b) in enumerate(component_pairs):
                here = pl.ds(x, 1)
                own_rows[t, m, here, :] = row_sum(fold(moved[a] * moved[b]))
                if a == b:
                    own_rows[t, 6 + m, here, :] = 2.0 * row_sum(fold(moved[a] * state[a]))
                else:
                    both = fold(moved[a] * state[b] + moved[b] * state[a])
                    own_rows[t, 6 + m, here, :] = row_sum(both)
                own_rows[t, 12 + m, here, :] = row_sum(fold(state[a] * state[b]))

    for copies in (halo_copies, flow_copies, sum_copies, edge_copies):
        for copy in copies:
            copy.wait_send()
    for copy in moment_copies:
        copy.wait_recv()
        copy.wait_send()


def finish_kernel(
    n_gy,
    counts_hbm,
    helper_hbm,
    start,
    drifted,
    extra,
    own_total,
    own_rows,
    moment_recv,
    base_out,
    extra_out,
    stress_out,
    counts,
    helper,
    base,
    stress,
    staged,
    relax,
    tile_sem,
    out_sem,
):
    gy = lax.axis_index("gy")
    helper_copy = pltpu.make_async_copy(helper_hbm, helper, out_sem.at[2])
    counts_copy = pltpu.make_async_copy(counts_hbm, counts, out_sem.at[3])
    extra_copy = pltpu.make_async_copy(extra, extra_out, out_sem.at[0])
    helper_copy.start()
    counts_copy.start()
    extra_copy.start()
    helper_copy.wait()
    counts_copy.wait()
    slots = [helper_slots(helper, gy, n_gy, t) for t in range(TILES)]
    tile_counts = [jnp.full((CHUNKS, LANES), counts[t], jnp.int32).astype(F32) for t in range(TILES)]
    for t in range(TILES):
        slot, hit = slots[t]
        total = own_total[t] + jnp.where(hit == 1, moment_recv[slot, 6], 0.0)
        relax[t] = relaxation(total, tile_counts[t])

    @pl.loop(0, TILES)
    def _(t):
        for x in range(CHUNKS):
            lanes = pl.ds(x * LANES, LANES)
            rate = wide(relax[t, pl.ds(x, 1), :])
            for c in range(3):
                base[t, c, :, lanes] = drifted[t, c, :, lanes] - rate * start[t, c, :, lanes]
        pltpu.make_async_copy(base.at[t], base_out.at[t], tile_sem.at[t]).start()

    for t in range(TILES):
        slot, hit = slots[t]
        rate = relax[t]
        second = []
        for m in range(6):
            own = own_rows[t, m] - rate * (own_rows[t, 6 + m] - rate * own_rows[t, 12 + m])
            second.append((own + jnp.where(hit == 1, moment_recv[slot, m], 0.0)) / tile_counts[t])
        trace = second[0] + second[1] + second[2]
        stretch = 1.0 / (1.0 - trace / max_extension)
        for m in range(6):
            staged[m, :, t, :] = (stretch * second[m] - (1.0 if m < 3 else 0.0)) / weissenberg

    for m in range(6):
        for x in range(CHUNKS):
            stress[m, :, pl.ds(x * LANES, LANES)] = staged[m, x]

    stress_copy = pltpu.make_async_copy(stress, stress_out, out_sem.at[1])
    stress_copy.start()
    for t in range(TILES):
        pltpu.make_async_copy(base.at[t], base_out.at[t], tile_sem.at[t]).wait()
    extra_copy.wait()
    stress_copy.wait()


def hold(array):
    return pltpu.with_memory_space_constraint(array, pltpu.HBM)


def solution(mesh):
    n_gx, n_gy = mesh.shape["gx"], mesh.shape["gy"]

    def per_device(
        velocity,
        wall_cells,
        tile_counts,
        helper_tile,
        base_fields,
        extra_fields,
        base_noise,
        extra_noise,
    ):
        hbm = pl.BlockSpec(memory_space=pltpu.HBM)
        vmem = pl.BlockSpec(memory_space=pltpu.VMEM)
        dma = pltpu.SemaphoreType.DMA
        counts = hold(tile_counts.reshape(TILES))
        helper = hold(helper_tile.reshape(n_gy))

        def block(*lead):
            return pltpu.VMEM((*lead, CHUNKS, LANES), F32)

        passed = pl.pallas_call(
            functools.partial(exchange_kernel, n_gx, n_gy),
            out_shape=(
                jax.ShapeDtypeStruct((TILES, 3, BASE, CELLS), F32),
                jax.ShapeDtypeStruct((TILES, 3, BASE, CELLS), F32),
                jax.ShapeDtypeStruct((3, EXTRA, CELLS), F32),
                jax.ShapeDtypeStruct((TILES, CHUNKS, LANES), F32),
                jax.ShapeDtypeStruct((TILES, 18, CHUNKS, LANES), F32),
                jax.ShapeDtypeStruct((n_gy, 7, CHUNKS, LANES), F32),
            ),
            in_specs=[hbm] * 8,
            out_specs=(vmem,) * 6,
            scratch_shapes=[
                pltpu.SMEM((TILES,), jnp.int32),
                pltpu.SMEM((n_gy,), jnp.int32),
                block(3, 8),
                pltpu.VMEM((8, 8, LANES), jnp.int32),
                pltpu.VMEM((TILES, 3, BASE, CELLS), jnp.bfloat16),
                pltpu.VMEM((TILES, 3, BASE, CELLS), jnp.bfloat16),
                pltpu.VMEM((STEPS, 3, EXTRA, CELLS), jnp.bfloat16),
                block(2, 3),
                block(8),
                block(6),
                block(TILES, 16),
                block(TILES),
                block(TILES, 5),
                block(n_gy, 5),
                block(n_gy, 5),
                block(TILES),
                block(),
                block(n_gy, 2),
                block(n_gy, 2),
                block(TILES, 3),
                block(n_gy, 3),
                block(n_gy, 3),
                block(45),
                block(18),
                block(TILES, 9),
                block(TILES),
                dma((9,)),
                dma((TILES,)),
                dma((4,)),
                dma((4,)),
                dma((n_gy,)),
                dma((n_gy,)),
                dma((n_gy,)),
                dma((n_gy,)),
                dma((n_gy,)),
                dma((n_gy,)),
                dma((n_gy,)),
                dma((n_gy,)),
                pltpu.SemaphoreType.REGULAR,
            ],
            compiler_params=pltpu.CompilerParams(
                collective_id=0, has_side_effects=True, vmem_limit_bytes=40 << 20
            ),
        )(
            counts,
            helper,
            hold(velocity),
            hold(wall_cells),
            hold(base_fields.reshape(TILES, 3, BASE, CELLS)),
            hold(extra_fields.reshape(3, EXTRA, CELLS)),
            hold(base_noise.reshape(TILES, STEPS, 3, BASE, CELLS)),
            hold(extra_noise.reshape(STEPS, 3, EXTRA, CELLS)),
        )
        base_out, extra_out, stress_out = pl.pallas_call(
            functools.partial(finish_kernel, n_gy),
            out_shape=(
                jax.ShapeDtypeStruct((TILES, 3, BASE, CELLS), F32),
                jax.ShapeDtypeStruct((3, EXTRA, CELLS), F32),
                jax.ShapeDtypeStruct((6, TILES, CELLS), F32),
            ),
            in_specs=[hbm] * 2 + [vmem] * 6,
            out_specs=(hbm,) * 3,
            scratch_shapes=[
                pltpu.SMEM((TILES,), jnp.int32),
                pltpu.SMEM((n_gy,), jnp.int32),
                pltpu.VMEM((TILES, 3, BASE, CELLS), F32),
                pltpu.VMEM((6, TILES, CELLS), F32),
                pltpu.VMEM((6, CHUNKS, TILES, LANES), F32),
                block(TILES),
                dma((TILES,)),
                dma((4,)),
            ],
            compiler_params=pltpu.CompilerParams(vmem_limit_bytes=40 << 20),
        )(counts, helper, *passed)
        return base_out[None, None], extra_out[None, None], stress_out.transpose(1, 0, 2)[None, None]

    in_specs = (
        P(None, "gx", "gy", None),
        P("gx", "gy", None),
        P("gx", "gy", None),
        P("gx", None),
        P("gx", "gy", None, None, None, None),
        P("gx", "gy", None, None, None),
        P("gx", "gy", None, None, None, None, None),
        P("gx", "gy", None, None, None, None),
    )
    out_specs = (
        P("gx", "gy", None, None, None, None),
        P("gx", "gy", None, None, None),
        P("gx", "gy", None, None, None),
    )
    return jax.shard_map(
        per_device, mesh=mesh, in_specs=in_specs, out_specs=out_specs, check_vma=False
    )
```

```python
import functools

import jax
import jax.numpy as jnp
from jax import lax
from jax.experimental import pallas as pl
from jax.experimental.pallas import tpu as pltpu
from jax.sharding import PartitionSpec as P

MESH = pl.DeviceIdType.MESH
F32 = jnp.float32

STEPS = 2
TILES = 8
CELLS = 1024
LANES = 128
CHUNKS = CELLS // LANES
BASE = 32
EXTRA = 224
GROUP = 32
HALF = 16

time_step = 0.05
weissenberg = 0.25
max_extension = 50.0
noise_scale = (time_step / weissenberg) ** 0.5
relax_scale = time_step * (0.5 / weissenberg)
component_pairs = ((0, 0), (1, 1), (2, 2), (0, 1), (0, 2), (1, 2))
early_pairs = [(i, j) for j in range(6) for i in range(j + 1)]
late_pairs = [(i, j) for j in range(6, 9) for i in range(j + 1)]
moment_at = {pair: n for n, pair in enumerate(early_pairs + late_pairs)}


def wide(row):
    return jnp.broadcast_to(row, (GROUP, LANES))


def matrix(grad_row, keep_row):
    keep = wide(keep_row)
    rows = []
    for a in range(3):
        row = [wide(grad_row(3 * a + b)) for b in range(3)]
        row[a] = row[a] + keep
        rows.append(row)
    return rows


def advance(mat, state, noise):
    return [
        mat[a][0] * state[0]
        + mat[a][1] * state[1]
        + mat[a][2] * state[2]
        + noise_scale * noise[a].astype(F32)
        for a in range(3)
    ]


def fold(block):
    out = block[:8]
    for k in range(1, block.shape[0] // 8):
        out = out + block[8 * k : 8 * k + 8]
    return out


def inner(left, right):
    return fold(left[0] * right[0] + left[1] * right[1] + left[2] * right[2])


def products(state):
    return [fold(state[a] * state[b]) for a, b in component_pairs]


def row_sum(block):
    return jnp.sum(block, axis=0, keepdims=True)


def relaxation(total, count):
    return relax_scale * (1.0 / (1.0 - total / count / max_extension))


SIDE = 4
offsets = sorted(
    range(1, SIDE * SIDE), key=lambda k: -sum(min(v, SIDE - v) for v in divmod(k, SIDE))
)


def wrap(value):
    return lax.rem(value + SIDE, SIDE)


def shifted(gy, k):
    x, y = gy // SIDE, lax.rem(gy, SIDE)
    return wrap(x + k // SIDE) * SIDE + wrap(y + k % SIDE)


def slot_from(gy, sender):
    x, y = gy // SIDE, lax.rem(gy, SIDE)
    return wrap(x - sender // SIDE) * SIDE + wrap(y - lax.rem(sender, SIDE))


def helper_slots(helper, gy, n_gy, t):
    slot, hit = jnp.int32(0), jnp.int32(0)
    for h in range(n_gy):
        match = helper[h] == gy * TILES + t
        slot = jnp.where(match, slot_from(gy, h), slot)
        hit = jnp.where(match, 1, hit)
    return slot, hit


def swap_blocks(regs, block):
    for bit in (1, 2, 4):
        upper = (block & bit) != 0
        new = list(regs)
        for i in range(8):
            if i & bit:
                continue
            j = i | bit
            new[i] = jnp.where(upper, pltpu.roll(regs[j], 16 * bit, 1), regs[i])
            new[j] = jnp.where(upper, regs[j], pltpu.roll(regs[i], LANES - 16 * bit, 1))
        regs = new
    return regs


def gradient(velocity, z_edge, fluid, y_edge, x_edge, sub, lane):
    deep = lane % 16

    def turn(value, shift):
        shift = shift % LANES
        return pltpu.roll(value, shift, 1) if shift else value

    grads = []
    for a in range(3):
        v = velocity[a]
        low = jnp.broadcast_to(x_edge[a : a + 1], (8, LANES))
        high = jnp.broadcast_to(x_edge[3 + a : 4 + a], (8, LANES))
        before = jnp.where(sub == 0, low, pltpu.roll(v, 1, 0))
        after = jnp.where(sub == 7, high, pltpu.roll(v, 7, 0))
        grads.append((after - before) * fluid)
        before = jnp.where(lane < 16, turn(y_edge, -16 * a), turn(v, 16))
        after = jnp.where(lane >= 112, turn(y_edge, 16 * (4 - a)), turn(v, -16))
        grads.append((after - before) * fluid)
        before = jnp.where(deep == 0, turn(z_edge, -a), turn(v, 1))
        after = jnp.where(deep == 15, turn(z_edge, a), turn(v, -1))
        grads.append((after - before) * fluid)
    return grads


def exchange_kernel(
    n_gx,
    n_gy,
    counts_hbm,
    helper_hbm,
    vel_hbm,
    wall_hbm,
    base_hbm,
    extra_hbm,
    base_noise_hbm,
    extra_noise_hbm,
    base,
    drifted,
    extra,
    own_total,
    own_rows,
    moment_recv,
    counts,
    helper,
    vel,
    wall,
    base_noise,
    late_noise,
    extra_noise,
    y_send,
    x_halo,
    y_halo,
    second,
    layer_own,
    flow_own,
    flow_send,
    flow_recv,
    sum_own,
    extra_sum,
    sum_recv,
    edge_own,
    edge_send,
    edge_recv,
    extra_second,
    helper_map,
    tile_grad,
    relax,
    in_sem,
    tile_sem,
    halo_send_sem,
    halo_recv_sem,
    flow_send_sem,
    flow_recv_sem,
    sum_send_sem,
    sum_recv_sem,
    edge_send_sem,
    edge_recv_sem,
    moment_send_sem,
    moment_recv_sem,
    ring_sem,
):
    gx = lax.axis_index("gx")
    gy = lax.axis_index("gy")
    up_x, down_x = lax.rem(gx + 1, n_gx), lax.rem(gx + n_gx - 1, n_gx)
    up_y, down_y = lax.rem(gy + 1, n_gy), lax.rem(gy + n_gy - 1, n_gy)

    barrier = pltpu.get_barrier_semaphore()
    near = [(gx, up_y), (gx, down_y), (up_x, gy), (down_x, gy)]
    near += [(gx, shifted(gy, v)) for v in range(1, SIDE)]
    near += [(gx, shifted(gy, v * SIDE)) for v in range(1, SIDE)]
    for device in near:
        pl.semaphore_signal(barrier, inc=1, device_id=device, device_id_type=MESH)

    vel_copy = pltpu.make_async_copy(vel_hbm, vel, in_sem.at[0])
    wall_copy = pltpu.make_async_copy(wall_hbm, wall, in_sem.at[1])
    helper_copy = pltpu.make_async_copy(helper_hbm, helper, in_sem.at[7])
    counts_copy = pltpu.make_async_copy(counts_hbm, counts, in_sem.at[8])
    extra_copy = pltpu.make_async_copy(extra_hbm, extra, in_sem.at[2])
    base_copies = [
        pltpu.make_async_copy(base_hbm.at[t], base.at[t], tile_sem.at[t]) for t in range(TILES)
    ]
    base_noise_copies = [
        pltpu.make_async_copy(base_noise_hbm.at[:, 0], base_noise, in_sem.at[3]),
        pltpu.make_async_copy(base_noise_hbm.at[:, 1], late_noise, in_sem.at[4]),
    ]
    extra_noise_copies = [
        pltpu.make_async_copy(extra_noise_hbm.at[s], extra_noise.at[s], in_sem.at[5 + s])
        for s in range(STEPS)
    ]
    vel_copy.start()
    wall_copy.start()
    helper_copy.start()
    counts_copy.start()
    for copy in base_copies:
        copy.start()
    base_noise_copies[0].start()
    extra_copy.start()
    extra_noise_copies[0].start()
    extra_noise_copies[1].start()
    base_noise_copies[1].start()

    def send_all(src_of, dst_of, send_sem, recv_sem):
        copies = [
            pltpu.make_async_remote_copy(
                src_ref=src_of(k),
                dst_ref=dst_of(k),
                send_sem=send_sem(k),
                recv_sem=recv_sem(k),
                device_id=(gx, shifted(gy, k)),
                device_id_type=MESH,
            )
            for k in offsets
        ]
        for copy in copies:
            copy.start()
        return copies

    sub = lax.broadcasted_iota(jnp.int32, (8, LANES), 0)
    lane = lax.broadcasted_iota(jnp.int32, (8, LANES), 1)
    block = lane // 16
    deep = lane % 16
    vel_copy.wait()
    for c in range(3):
        y_send[0, c] = vel[c, :, 7, :]
        y_send[1, c] = vel[c, :, 0, :]
    pl.semaphore_wait(barrier, len(near))

    halo_copies = [
        pltpu.make_async_remote_copy(
            src_ref=src,
            dst_ref=dst,
            send_sem=halo_send_sem.at[i],
            recv_sem=halo_recv_sem.at[i],
            device_id=device,
            device_id_type=MESH,
        )
        for i, (src, dst, device) in enumerate(
            (
                (y_send.at[0], y_halo.at[0:3], (gx, up_y)),
                (y_send.at[1], y_halo.at[3:6], (gx, down_y)),
                (vel.at[:, 7], x_halo.at[0:3], (up_x, gy)),
                (vel.at[:, 0], x_halo.at[3:6], (down_x, gy)),
            )
        )
    ]
    for copy in halo_copies:
        copy.start()
    for v in range(1, SIDE):
        pl.semaphore_signal(
            ring_sem, inc=1, device_id=(gx, shifted(gy, v)), device_id_type=MESH
        )
    x_halo[6:] = jnp.zeros((2, 8, LANES), F32)
    flow = [swap_blocks([vel[a, :, y, :] for y in range(8)], block) for a in range(3)]
    for t in range(TILES):
        z_edge = jnp.zeros((8, LANES), F32)
        for a in range(3):
            if t > 0:
                z_edge = jnp.where(deep == a, pltpu.roll(flow[a][t - 1], 113 + a, 1), z_edge)
            if t < TILES - 1:
                z_edge = jnp.where(deep == 15 - a, pltpu.roll(flow[a][t + 1], 15 - a, 1), z_edge)
            flow_own[t, a] = flow[a][t]
        flow_own[t, 3] = z_edge
    wall_copy.wait()
    fluid = swap_blocks(
        [jnp.where(wall[:, y, :] == 0, 0.5 * time_step, 0.0).astype(F32) for y in range(8)], block
    )
    for t in range(TILES):
        flow_own[t, 4] = fluid[t]
    sides = [y_send[0, a] for a in range(3)] + [y_send[1, a] for a in range(3)]
    layers = swap_blocks(sides + [jnp.zeros((8, LANES), F32)] * 2, block)
    for t in range(TILES):
        layer_own[t] = layers[t]
    helper_copy.wait()
    counts_copy.wait()

    named = [helper[shifted(gy, k)] for k in range(n_gy)]
    wanted = [lax.rem(name, TILES) for name in named]
    for k in range(n_gy):
        mine = named[k] // TILES == gy
        flow_send[k, 0] = jnp.where(mine, flow_own[wanted[k], 0], layer_own[wanted[k]])
        flow_send[k, 1:] = flow_own[wanted[k], 1:]

    pl.semaphore_wait(ring_sem, SIDE - 1)
    flow_copies = send_all(
        lambda k: flow_send.at[k],
        lambda k: flow_recv.at[k],
        lambda k: flow_send_sem.at[k],
        lambda k: flow_recv_sem.at[k],
    )
    flow_recv[0] = flow_send[0]

    owner = helper[gy] // TILES
    my_slot = slot_from(gy, owner)
    low_slot = slot_from(gy, lax.rem(owner + n_gy - 1, n_gy))
    high_slot = slot_from(gy, lax.rem(owner + 1, n_gy))
    slots = [helper_slots(helper, gy, n_gy, t) for t in range(TILES)]

    for copy in base_copies:
        copy.wait()
    base_noise_copies[0].wait()

    @pl.loop(0, TILES)
    def _(t):
        for x in range(CHUNKS):
            lanes = pl.ds(x * LANES, LANES)
            state = [base[t, c, :, lanes] for c in range(3)]
            noise = [base_noise[t, c, :, lanes].astype(F32) for c in range(3)]
            for m, total in enumerate(products(state)):
                second[t, m, pl.ds(x, 1), :] = row_sum(total)
            for a in range(3):
                for b in range(3):
                    second[t, 6 + 3 * a + b, pl.ds(x, 1), :] = row_sum(fold(state[a] * noise[b]))
            second[t, 15, pl.ds(x, 1), :] = row_sum(inner(noise, noise))

    for t in range(TILES):
        sum_own[t] = second[t, 0] + second[t, 1] + second[t, 2]

    for copy in halo_copies:
        copy.wait_recv()
    low = jnp.where(gx > 0, 1.0, 0.0)
    high = jnp.where(gx < n_gx - 1, 1.0, 0.0)
    inside = jnp.where(sub < 3, low, high)
    x_edges = swap_blocks([x_halo[:, y, :] * inside for y in range(8)], block)
    sides = [jnp.where(gy > 0, y_halo[a], 0.0) for a in range(3)]
    sides += [jnp.where(gy < n_gy - 1, y_halo[3 + a], 0.0) for a in range(3)]
    sides += [jnp.zeros((8, LANES), F32)] * 2
    y_edges = swap_blocks(sides, block)
    for t in range(TILES):
        layer_own[t] = y_edges[t]
        edge_own[t, 0] = x_edges[t]

    for t in range(TILES):
        grads = gradient(
            [flow_own[t, a] for a in range(3)],
            flow_own[t, 3],
            flow_own[t, 4],
            layer_own[t],
            edge_own[t, 0],
            sub,
            lane,
        )
        for c in range(9):
            tile_grad[t, c] = grads[c]
        mat = [[grads[3 * a + b] + (1.0 if a == b else 0.0) for b in range(3)] for a in range(3)]
        pairs = {}
        for m, (a, b) in enumerate(component_pairs):
            pairs[a, b] = pairs[b, a] = second[t, m]
        cross = [[second[t, 6 + 3 * a + b] for b in range(3)] for a in range(3)]
        once = noise_scale * (cross[0][0] + cross[1][1] + cross[2][2])
        twice = (noise_scale * noise_scale) * second[t, 15]
        for a in range(3):
            for b in range(3):
                inner_row = (
                    mat[a][0] * pairs[0, b] + mat[a][1] * pairs[1, b] + mat[a][2] * pairs[2, b]
                )
                once = once + (mat[a][b] * pairs[a, b])
                twice = twice + mat[a][b] * (inner_row + (2.0 * noise_scale) * cross[b][a])
        edge_own[t, 1] = once
        edge_own[t, 2] = twice
        edge_own[t, 3] = sum_own[t]

    for k in range(n_gy):
        edge_send[k] = edge_own[wanted[k]]

    edge_copies = send_all(
        lambda k: edge_send.at[k],
        lambda k: edge_recv.at[k],
        lambda k: edge_send_sem.at[k],
        lambda k: edge_recv_sem.at[k],
    )
    edge_recv[0] = edge_send[0]

    extra_copy.wait()
    for copy in extra_noise_copies:
        copy.wait()
    for wanted_pairs in (early_pairs, late_pairs):

        @pl.loop(0, CHUNKS)
        def _(x):
            lanes = pl.ds(pl.multiple_of(x * LANES, LANES), LANES)
            totals = [jnp.zeros((8, LANES), F32) for _ in wanted_pairs]
            for f in range(EXTRA // HALF):
                fields = pl.ds(f * HALF, HALF)
                parts = [extra[c, fields, lanes] for c in range(3)]
                for s in range(STEPS):
                    parts += [extra_noise[s, c, fields, lanes].astype(F32) for c in range(3)]
                totals = [
                    total + fold(parts[i] * parts[j])
                    for total, (i, j) in zip(totals, wanted_pairs)
                ]
            for pair, total in zip(wanted_pairs, totals):
                extra_second[moment_at[pair], pl.ds(x, 1), :] = row_sum(total)

        if wanted_pairs is early_pairs:
            extra_sum[...] = (
                extra_second[moment_at[0, 0]]
                + extra_second[moment_at[1, 1]]
                + extra_second[moment_at[2, 2]]
            )
            sum_copies = send_all(
                lambda k: extra_sum,
                lambda k: sum_recv.at[k],
                lambda k: sum_send_sem.at[k],
                lambda k: sum_recv_sem.at[k],
            )
            sum_recv[0] = extra_sum[...]

    for copies in (flow_copies, edge_copies):
        for copy in copies:
            copy.wait_recv()
    grads = gradient(
        [flow_recv[my_slot, a] for a in range(3)],
        flow_recv[my_slot, 3],
        flow_recv[my_slot, 4],
        jnp.where(
            block < 3,
            jnp.where(owner > 0, flow_recv[low_slot, 0], 0.0),
            jnp.where(owner < n_gy - 1, flow_recv[high_slot, 0], 0.0),
        ),
        edge_recv[my_slot, 0],
        sub,
        lane,
    )
    first = edge_recv[my_slot, 3]
    rate = relaxation(first + extra_sum[...], 256.0)
    own_share = edge_recv[my_slot, 2] - rate * (2.0 * edge_recv[my_slot, 1] - rate * first)

    def pair_sum(i, j):
        return extra_second[moment_at[min(i, j), max(i, j)]]

    def step_matrix(keep):
        return [
            [grads[3 * a + b] + keep if a == b else grads[3 * a + b] for b in range(3)]
            for a in range(3)
        ]

    def dot(left, right):
        out = left[0] * right[0]
        for u, v in zip(left[1:], right[1:]):
            out = out + u * v
        return out

    one = step_matrix(1.0 - rate)
    total = jnp.zeros((8, LANES), F32)
    for a in range(3):
        mixed = [
            dot(one[a], [pair_sum(i, j) for i in range(3)]) + noise_scale * pair_sum(3 + a, j)
            for j in (0, 1, 2, 3 + a)
        ]
        total = total + dot(one[a], mixed[:3]) + noise_scale * mixed[3]
    moment_recv[0, 6] = total
    two = step_matrix(1.0 - relaxation(total + own_share, 256.0))
    combined = []
    for a in range(3):
        row = [dot(two[a], [one[c][b] for c in range(3)]) for b in range(3)]
        row += [noise_scale * two[a][b] for b in range(3)]
        combined.append(row)
        for b in range(6):
            helper_map[6 * a + b] = row[b]
    for a in range(3):
        mixed = [
            dot(combined[a], [pair_sum(i, j) for i in range(6)]) + noise_scale * pair_sum(6 + a, j)
            for j in range(9)
        ]
        for m, (first_axis, second_axis) in enumerate(component_pairs):
            if first_axis == a:
                moment_recv[0, m] = (
                    dot(combined[second_axis], mixed[:6]) + noise_scale * mixed[6 + second_axis]
                )

    moment_copies = send_all(
        lambda k: moment_recv.at[0],
        lambda k: moment_recv.at[k],
        lambda k: moment_send_sem.at[k],
        lambda k: moment_recv_sem.at[k],
    )

    @pl.loop(0, CHUNKS)
    def _(x):
        lanes = pl.ds(pl.multiple_of(x * LANES, LANES), LANES)
        rows = [
            jnp.broadcast_to(helper_map[n, pl.ds(x, 1), :], (HALF, LANES)) for n in range(18)
        ]
        for f in range(EXTRA // HALF):
            fields = pl.ds(f * HALF, HALF)
            parts = [extra[c, fields, lanes] for c in range(3)]
            parts += [extra_noise[0, c, fields, lanes].astype(F32) for c in range(3)]
            for a in range(3):
                last = extra_noise[1, a, fields, lanes].astype(F32)
                extra[a, fields, lanes] = dot(rows[6 * a : 6 * a + 6], parts) + noise_scale * last

    for copy in sum_copies:
        copy.wait_recv()
    for t in range(TILES):
        slot, hit = slots[t]
        count = jnp.full((CHUNKS, LANES), counts[t], jnp.int32).astype(F32)
        total = sum_own[t] + jnp.where(hit == 1, sum_recv[slot], 0.0)
        rate = relaxation(total, count)
        relax[t] = rate
        own_total[t] = edge_own[t, 2] - rate * (2.0 * edge_own[t, 1] - rate * sum_own[t])

    base_noise_copies[1].wait()

    @pl.loop(0, TILES)
    def _(t):
        for x in range(CHUNKS):
            lanes = pl.ds(x * LANES, LANES)
            mat = matrix(lambda c: tile_grad[t, c, pl.ds(x, 1), :], jnp.ones((1, LANES), F32))
            rate = wide(relax[t, pl.ds(x, 1), :])
            start = [base[t, c, :, lanes] for c in range(3)]
            state = advance(mat, start, [base_noise[t, c, :, lanes] for c in range(3)])
            state = [state[c] - rate * start[c] for c in range(3)]
            for c in range(3):
                base[t, c, :, lanes] = state[c]
            moved = advance(mat, state, [late_noise[t, c, :, lanes] for c in range(3)])
            for c in range(3):
                drifted[t, c, :, lanes] = moved[c]
            for m, (a, b) in enumerate(component_pairs):
                here = pl.ds(x, 1)
                own_rows[t, m, here, :] = row_sum(fold(moved[a] * moved[b]))
                if a == b:
                    own_rows[t, 6 + m, here, :] = 2.0 * row_sum(fold(moved[a] * state[a]))
                else:
                    both = fold(moved[a] * state[b] + moved[b] * state[a])
                    own_rows[t, 6 + m, here, :] = row_sum(both)
                own_rows[t, 12 + m, here, :] = row_sum(fold(state[a] * state[b]))

    for copies in (halo_copies, flow_copies, sum_copies, edge_copies):
        for copy in copies:
            copy.wait_send()
    for copy in moment_copies:
        copy.wait_recv()
        copy.wait_send()


def finish_kernel(
    n_gy,
    counts_hbm,
    helper_hbm,
    start,
    drifted,
    extra,
    own_total,
    own_rows,
    moment_recv,
    base_out,
    extra_out,
    stress_out,
    counts,
    helper,
    base,
    stress,
    staged,
    relax,
    tile_sem,
    out_sem,
):
    gy = lax.axis_index("gy")
    helper_copy = pltpu.make_async_copy(helper_hbm, helper, out_sem.at[2])
    counts_copy = pltpu.make_async_copy(counts_hbm, counts, out_sem.at[3])
    extra_copy = pltpu.make_async_copy(extra, extra_out, out_sem.at[0])
    helper_copy.start()
    counts_copy.start()
    extra_copy.start()
    helper_copy.wait()
    counts_copy.wait()
    slots = [helper_slots(helper, gy, n_gy, t) for t in range(TILES)]
    tile_counts = [jnp.full((CHUNKS, LANES), counts[t], jnp.int32).astype(F32) for t in range(TILES)]
    for t in range(TILES):
        slot, hit = slots[t]
        total = own_total[t] + jnp.where(hit == 1, moment_recv[slot, 6], 0.0)
        relax[t] = relaxation(total, tile_counts[t])

    @pl.loop(0, TILES)
    def _(t):
        for x in range(CHUNKS):
            lanes = pl.ds(x * LANES, LANES)
            rate = wide(relax[t, pl.ds(x, 1), :])
            for c in range(3):
                base[t, c, :, lanes] = drifted[t, c, :, lanes] - rate * start[t, c, :, lanes]
        pltpu.make_async_copy(base.at[t], base_out.at[t], tile_sem.at[t]).start()

    for t in range(TILES):
        slot, hit = slots[t]
        rate = relax[t]
        second = []
        for m in range(6):
            own = own_rows[t, m] - rate * (own_rows[t, 6 + m] - rate * own_rows[t, 12 + m])
            second.append((own + jnp.where(hit == 1, moment_recv[slot, m], 0.0)) / tile_counts[t])
        trace = second[0] + second[1] + second[2]
        stretch = 1.0 / (1.0 - trace / max_extension)
        for m in range(6):
            staged[m, :, t, :] = (stretch * second[m] - (1.0 if m < 3 else 0.0)) / weissenberg

    for m in range(6):
        for x in range(CHUNKS):
            stress[m, :, pl.ds(x * LANES, LANES)] = staged[m, x]

    stress_copy = pltpu.make_async_copy(stress, stress_out, out_sem.at[1])
    stress_copy.start()
    for t in range(TILES):
        pltpu.make_async_copy(base.at[t], base_out.at[t], tile_sem.at[t]).wait()
    extra_copy.wait()
    stress_copy.wait()


def hold(array):
    return pltpu.with_memory_space_constraint(array, pltpu.HBM)


def solution(mesh):
    n_gx, n_gy = mesh.shape["gx"], mesh.shape["gy"]

    def per_device(
        velocity,
        wall_cells,
        tile_counts,
        helper_tile,
        base_fields,
        extra_fields,
        base_noise,
        extra_noise,
    ):
        hbm = pl.BlockSpec(memory_space=pltpu.HBM)
        vmem = pl.BlockSpec(memory_space=pltpu.VMEM)
        dma = pltpu.SemaphoreType.DMA
        counts = hold(tile_counts.reshape(TILES))
        helper = hold(helper_tile.reshape(n_gy))

        def block(*lead):
            return pltpu.VMEM((*lead, CHUNKS, LANES), F32)

        passed = pl.pallas_call(
            functools.partial(exchange_kernel, n_gx, n_gy),
            out_shape=(
                jax.ShapeDtypeStruct((TILES, 3, BASE, CELLS), F32),
                jax.ShapeDtypeStruct((TILES, 3, BASE, CELLS), F32),
                jax.ShapeDtypeStruct((3, EXTRA, CELLS), F32),
                jax.ShapeDtypeStruct((TILES, CHUNKS, LANES), F32),
                jax.ShapeDtypeStruct((TILES, 18, CHUNKS, LANES), F32),
                jax.ShapeDtypeStruct((n_gy, 7, CHUNKS, LANES), F32),
            ),
            in_specs=[hbm] * 8,
            out_specs=(vmem,) * 6,
            scratch_shapes=[
                pltpu.SMEM((TILES,), jnp.int32),
                pltpu.SMEM((n_gy,), jnp.int32),
                block(3, 8),
                pltpu.VMEM((8, 8, LANES), jnp.int32),
                pltpu.VMEM((TILES, 3, BASE, CELLS), jnp.bfloat16),
                pltpu.VMEM((TILES, 3, BASE, CELLS), jnp.bfloat16),
                pltpu.VMEM((STEPS, 3, EXTRA, CELLS), jnp.bfloat16),
                block(2, 3),
                block(8),
                block(6),
                block(TILES, 16),
                block(TILES),
                block(TILES, 5),
                block(n_gy, 5),
                block(n_gy, 5),
                block(TILES),
                block(),
                block(n_gy),
                block(TILES, 4),
                block(n_gy, 4),
                block(n_gy, 4),
                block(45),
                block(18),
                block(TILES, 9),
                block(TILES),
                dma((9,)),
                dma((TILES,)),
                dma((4,)),
                dma((4,)),
                dma((n_gy,)),
                dma((n_gy,)),
                dma((n_gy,)),
                dma((n_gy,)),
                dma((n_gy,)),
                dma((n_gy,)),
                dma((n_gy,)),
                dma((n_gy,)),
                pltpu.SemaphoreType.REGULAR,
            ],
            compiler_params=pltpu.CompilerParams(
                collective_id=0, has_side_effects=True, vmem_limit_bytes=40 << 20
            ),
        )(
            counts,
            helper,
            hold(velocity),
            hold(wall_cells),
            hold(base_fields.reshape(TILES, 3, BASE, CELLS)),
            hold(extra_fields.reshape(3, EXTRA, CELLS)),
            hold(base_noise.reshape(TILES, STEPS, 3, BASE, CELLS)),
            hold(extra_noise.reshape(STEPS, 3, EXTRA, CELLS)),
        )
        base_out, extra_out, stress_out = pl.pallas_call(
            functools.partial(finish_kernel, n_gy),
            out_shape=(
                jax.ShapeDtypeStruct((TILES, 3, BASE, CELLS), F32),
                jax.ShapeDtypeStruct((3, EXTRA, CELLS), F32),
                jax.ShapeDtypeStruct((6, TILES, CELLS), F32),
            ),
            in_specs=[hbm] * 2 + [vmem] * 6,
            out_specs=(hbm,) * 3,
            scratch_shapes=[
                pltpu.SMEM((TILES,), jnp.int32),
                pltpu.SMEM((n_gy,), jnp.int32),
                pltpu.VMEM((TILES, 3, BASE, CELLS), F32),
                pltpu.VMEM((6, TILES, CELLS), F32),
                pltpu.VMEM((6, CHUNKS, TILES, LANES), F32),
                block(TILES),
                dma((TILES,)),
                dma((4,)),
            ],
            compiler_params=pltpu.CompilerParams(vmem_limit_bytes=40 << 20),
        )(counts, helper, *passed)
        return base_out[None, None], extra_out[None, None], stress_out.transpose(1, 0, 2)[None, None]

    in_specs = (
        P(None, "gx", "gy", None),
        P("gx", "gy", None),
        P("gx", "gy", None),
        P("gx", None),
        P("gx", "gy", None, None, None, None),
        P("gx", "gy", None, None, None),
        P("gx", "gy", None, None, None, None, None),
        P("gx", "gy", None, None, None, None),
    )
    out_specs = (
        P("gx", "gy", None, None, None, None),
        P("gx", "gy", None, None, None),
        P("gx", "gy", None, None, None),
    )
    return jax.shard_map(
        per_device, mesh=mesh, in_specs=in_specs, out_specs=out_specs, check_vma=False
    )
```

```python
import functools

import jax
import jax.numpy as jnp
from jax import lax
from jax.experimental import pallas as pl
from jax.experimental.pallas import tpu as pltpu
from jax.sharding import PartitionSpec as P

MESH = pl.DeviceIdType.MESH
F32 = jnp.float32

STEPS = 2
TILES = 8
CELLS = 1024
LANES = 128
CHUNKS = CELLS // LANES
BASE = 32
EXTRA = 224
GROUP = 32
HALF = 16

time_step = 0.05
weissenberg = 0.25
max_extension = 50.0
noise_scale = (time_step / weissenberg) ** 0.5
relax_scale = time_step * (0.5 / weissenberg)
component_pairs = ((0, 0), (1, 1), (2, 2), (0, 1), (0, 2), (1, 2))
early_pairs = [(i, j) for j in range(6) for i in range(j + 1)]
late_pairs = [(i, j) for j in range(6, 9) for i in range(j + 1)]
moment_at = {pair: n for n, pair in enumerate(early_pairs + late_pairs)}


def wide(row):
    return jnp.broadcast_to(row, (GROUP, LANES))


def matrix(grad_row, keep_row):
    keep = wide(keep_row)
    rows = []
    for a in range(3):
        row = [wide(grad_row(3 * a + b)) for b in range(3)]
        row[a] = row[a] + keep
        rows.append(row)
    return rows


def advance(mat, state, noise):
    return [
        mat[a][0] * state[0]
        + mat[a][1] * state[1]
        + mat[a][2] * state[2]
        + noise_scale * noise[a].astype(F32)
        for a in range(3)
    ]


def fold(block):
    out = block[:8]
    for k in range(1, block.shape[0] // 8):
        out = out + block[8 * k : 8 * k + 8]
    return out


def inner(left, right):
    return fold(left[0] * right[0] + left[1] * right[1] + left[2] * right[2])


def products(state):
    return [fold(state[a] * state[b]) for a, b in component_pairs]


def row_sum(block):
    return jnp.sum(block, axis=0, keepdims=True)


def relaxation(total, count):
    return relax_scale * (1.0 / (1.0 - total / count / max_extension))


SIDE = 4
offsets = sorted(
    range(1, SIDE * SIDE), key=lambda k: -sum(min(v, SIDE - v) for v in divmod(k, SIDE))
)


def wrap(value):
    return lax.rem(value + SIDE, SIDE)


def shifted(gy, k):
    x, y = gy // SIDE, lax.rem(gy, SIDE)
    return wrap(x + k // SIDE) * SIDE + wrap(y + k % SIDE)


def slot_from(gy, sender):
    x, y = gy // SIDE, lax.rem(gy, SIDE)
    return wrap(x - sender // SIDE) * SIDE + wrap(y - lax.rem(sender, SIDE))


def helper_slots(helper, gy, n_gy):
    place = [helper[h] - gy * TILES for h in range(n_gy)]
    sender = [slot_from(gy, h) for h in range(n_gy)]
    slots = []
    for t in range(TILES):
        slot = jnp.int32(-1)
        for h in range(n_gy):
            slot = jnp.where(place[h] == t, sender[h], slot)
        slots.append((jnp.maximum(slot, 0), slot >= 0))
    return slots


def swap_blocks(regs, block):
    for bit in (1, 2, 4):
        upper = (block & bit) != 0
        new = list(regs)
        for i in range(8):
            if i & bit:
                continue
            j = i | bit
            new[i] = jnp.where(upper, pltpu.roll(regs[j], 16 * bit, 1), regs[i])
            new[j] = jnp.where(upper, regs[j], pltpu.roll(regs[i], LANES - 16 * bit, 1))
        regs = new
    return regs


def gradient(velocity, z_edge, fluid, y_edge, x_edge, sub, lane):
    deep = lane % 16

    def turn(value, shift):
        shift = shift % LANES
        return pltpu.roll(value, shift, 1) if shift else value

    grads = []
    for a in range(3):
        v = velocity[a]
        low = jnp.broadcast_to(x_edge[a : a + 1], (8, LANES))
        high = jnp.broadcast_to(x_edge[3 + a : 4 + a], (8, LANES))
        before = jnp.where(sub == 0, low, pltpu.roll(v, 1, 0))
        after = jnp.where(sub == 7, high, pltpu.roll(v, 7, 0))
        grads.append((after - before) * fluid)
        before = jnp.where(lane < 16, turn(y_edge, -16 * a), turn(v, 16))
        after = jnp.where(lane >= 112, turn(y_edge, 16 * (4 - a)), turn(v, -16))
        grads.append((after - before) * fluid)
        before = jnp.where(deep == 0, turn(z_edge, -a), turn(v, 1))
        after = jnp.where(deep == 15, turn(z_edge, a), turn(v, -1))
        grads.append((after - before) * fluid)
    return grads


def exchange_kernel(
    n_gx,
    n_gy,
    counts_hbm,
    helper_hbm,
    vel_hbm,
    wall_hbm,
    base_hbm,
    extra_hbm,
    base_noise_hbm,
    extra_noise_hbm,
    base,
    drifted,
    extra,
    own_total,
    own_rows,
    moment_recv,
    counts,
    helper,
    vel,
    wall,
    base_noise,
    late_noise,
    extra_noise,
    y_send,
    x_halo,
    y_halo,
    second,
    layer_own,
    flow_own,
    flow_send,
    flow_recv,
    sum_own,
    extra_sum,
    sum_recv,
    edge_own,
    edge_send,
    edge_recv,
    extra_second,
    helper_map,
    tile_grad,
    relax,
    in_sem,
    tile_sem,
    halo_send_sem,
    halo_recv_sem,
    flow_send_sem,
    flow_recv_sem,
    sum_send_sem,
    sum_recv_sem,
    edge_send_sem,
    edge_recv_sem,
    moment_send_sem,
    moment_recv_sem,
    ring_sem,
):
    gx = lax.axis_index("gx")
    gy = lax.axis_index("gy")
    up_x, down_x = lax.rem(gx + 1, n_gx), lax.rem(gx + n_gx - 1, n_gx)
    up_y, down_y = lax.rem(gy + 1, n_gy), lax.rem(gy + n_gy - 1, n_gy)

    barrier = pltpu.get_barrier_semaphore()
    near = [(gx, up_y), (gx, down_y), (up_x, gy), (down_x, gy)]
    near += [(gx, shifted(gy, v)) for v in range(1, SIDE)]
    near += [(gx, shifted(gy, v * SIDE)) for v in range(1, SIDE)]
    for device in near:
        pl.semaphore_signal(barrier, inc=1, device_id=device, device_id_type=MESH)

    vel_copy = pltpu.make_async_copy(vel_hbm, vel, in_sem.at[0])
    wall_copy = pltpu.make_async_copy(wall_hbm, wall, in_sem.at[1])
    helper_copy = pltpu.make_async_copy(helper_hbm, helper, in_sem.at[7])
    counts_copy = pltpu.make_async_copy(counts_hbm, counts, in_sem.at[8])
    extra_copy = pltpu.make_async_copy(extra_hbm, extra, in_sem.at[2])
    base_copies = [
        pltpu.make_async_copy(base_hbm.at[t], base.at[t], tile_sem.at[t]) for t in range(TILES)
    ]
    base_noise_copies = [
        pltpu.make_async_copy(base_noise_hbm.at[:, 0], base_noise, in_sem.at[3]),
        pltpu.make_async_copy(base_noise_hbm.at[:, 1], late_noise, in_sem.at[4]),
    ]
    extra_noise_copies = [
        pltpu.make_async_copy(extra_noise_hbm.at[s], extra_noise.at[s], in_sem.at[5 + s])
        for s in range(STEPS)
    ]
    vel_copy.start()
    wall_copy.start()
    helper_copy.start()
    counts_copy.start()
    for copy in base_copies:
        copy.start()
    base_noise_copies[0].start()
    extra_copy.start()
    extra_noise_copies[0].start()
    extra_noise_copies[1].start()
    base_noise_copies[1].start()

    def send_all(src_of, dst_of, send_sem, recv_sem):
        copies = [
            pltpu.make_async_remote_copy(
                src_ref=src_of(k),
                dst_ref=dst_of(k),
                send_sem=send_sem(k),
                recv_sem=recv_sem(k),
                device_id=(gx, shifted(gy, k)),
                device_id_type=MESH,
            )
            for k in offsets
        ]
        for copy in copies:
            copy.start()
        return copies

    sub = lax.broadcasted_iota(jnp.int32, (8, LANES), 0)
    lane = lax.broadcasted_iota(jnp.int32, (8, LANES), 1)
    block = lane // 16
    deep = lane % 16
    vel_copy.wait()
    for c in range(3):
        y_send[0, c] = vel[c, :, 7, :]
        y_send[1, c] = vel[c, :, 0, :]
    pl.semaphore_wait(barrier, len(near))

    halo_copies = [
        pltpu.make_async_remote_copy(
            src_ref=src,
            dst_ref=dst,
            send_sem=halo_send_sem.at[i],
            recv_sem=halo_recv_sem.at[i],
            device_id=device,
            device_id_type=MESH,
        )
        for i, (src, dst, device) in enumerate(
            (
                (y_send.at[0], y_halo.at[0:3], (gx, up_y)),
                (y_send.at[1], y_halo.at[3:6], (gx, down_y)),
                (vel.at[:, 7], x_halo.at[0:3], (up_x, gy)),
                (vel.at[:, 0], x_halo.at[3:6], (down_x, gy)),
            )
        )
    ]
    for copy in halo_copies:
        copy.start()
    for v in range(1, SIDE):
        pl.semaphore_signal(
            ring_sem, inc=1, device_id=(gx, shifted(gy, v)), device_id_type=MESH
        )
    x_halo[6:] = jnp.zeros((2, 8, LANES), F32)
    flow = [swap_blocks([vel[a, :, y, :] for y in range(8)], block) for a in range(3)]
    for t in range(TILES):
        z_edge = jnp.zeros((8, LANES), F32)
        for a in range(3):
            if t > 0:
                z_edge = jnp.where(deep == a, pltpu.roll(flow[a][t - 1], 113 + a, 1), z_edge)
            if t < TILES - 1:
                z_edge = jnp.where(deep == 15 - a, pltpu.roll(flow[a][t + 1], 15 - a, 1), z_edge)
            flow_own[t, a] = flow[a][t]
        flow_own[t, 3] = z_edge
    wall_copy.wait()
    fluid = swap_blocks(
        [jnp.where(wall[:, y, :] == 0, 0.5 * time_step, 0.0).astype(F32) for y in range(8)], block
    )
    for t in range(TILES):
        flow_own[t, 4] = fluid[t]
    sides = [y_send[0, a] for a in range(3)] + [y_send[1, a] for a in range(3)]
    layers = swap_blocks(sides + [jnp.zeros((8, LANES), F32)] * 2, block)
    for t in range(TILES):
        layer_own[t] = layers[t]
    helper_copy.wait()
    counts_copy.wait()

    named = [helper[shifted(gy, k)] for k in range(n_gy)]
    wanted = [lax.rem(name, TILES) for name in named]
    for k in range(n_gy):
        mine = named[k] // TILES == gy
        flow_send[k, 0] = jnp.where(mine, flow_own[wanted[k], 0], layer_own[wanted[k]])
        flow_send[k, 1:] = flow_own[wanted[k], 1:]

    pl.semaphore_wait(ring_sem, SIDE - 1)
    flow_copies = send_all(
        lambda k: flow_send.at[k],
        lambda k: flow_recv.at[k],
        lambda k: flow_send_sem.at[k],
        lambda k: flow_recv_sem.at[k],
    )
    flow_recv[0] = flow_send[0]

    owner = helper[gy] // TILES
    my_slot = slot_from(gy, owner)
    low_slot = slot_from(gy, lax.rem(owner + n_gy - 1, n_gy))
    high_slot = slot_from(gy, lax.rem(owner + 1, n_gy))
    slots = helper_slots(helper, gy, n_gy)

    for copy in base_copies:
        copy.wait()
    base_noise_copies[0].wait()

    @pl.loop(0, TILES)
    def _(t):
        for x in range(CHUNKS):
            lanes = pl.ds(x * LANES, LANES)
            state = [base[t, c, :, lanes] for c in range(3)]
            noise = [base_noise[t, c, :, lanes].astype(F32) for c in range(3)]
            for m, total in enumerate(products(state)):
                second[t, m, pl.ds(x, 1), :] = row_sum(total)
            for a in range(3):
                for b in range(3):
                    second[t, 6 + 3 * a + b, pl.ds(x, 1), :] = row_sum(fold(state[a] * noise[b]))
            second[t, 15, pl.ds(x, 1), :] = row_sum(inner(noise, noise))

    for t in range(TILES):
        sum_own[t] = second[t, 0] + second[t, 1] + second[t, 2]

    for copy in halo_copies:
        copy.wait_recv()
    low = jnp.where(gx > 0, 1.0, 0.0)
    high = jnp.where(gx < n_gx - 1, 1.0, 0.0)
    inside = jnp.where(sub < 3, low, high)
    x_edges = swap_blocks([x_halo[:, y, :] * inside for y in range(8)], block)
    sides = [jnp.where(gy > 0, y_halo[a], 0.0) for a in range(3)]
    sides += [jnp.where(gy < n_gy - 1, y_halo[3 + a], 0.0) for a in range(3)]
    sides += [jnp.zeros((8, LANES), F32)] * 2
    y_edges = swap_blocks(sides, block)
    for t in range(TILES):
        layer_own[t] = y_edges[t]
        edge_own[t, 0] = x_edges[t]

    for t in range(TILES):
        grads = gradient(
            [flow_own[t, a] for a in range(3)],
            flow_own[t, 3],
            flow_own[t, 4],
            layer_own[t],
            edge_own[t, 0],
            sub,
            lane,
        )
        for c in range(9):
            tile_grad[t, c] = grads[c]
        mat = [[grads[3 * a + b] + (1.0 if a == b else 0.0) for b in range(3)] for a in range(3)]
        pairs = {}
        for m, (a, b) in enumerate(component_pairs):
            pairs[a, b] = pairs[b, a] = second[t, m]
        cross = [[second[t, 6 + 3 * a + b] for b in range(3)] for a in range(3)]
        once = noise_scale * (cross[0][0] + cross[1][1] + cross[2][2])
        twice = (noise_scale * noise_scale) * second[t, 15]
        for a in range(3):
            for b in range(3):
                inner_row = (
                    mat[a][0] * pairs[0, b] + mat[a][1] * pairs[1, b] + mat[a][2] * pairs[2, b]
                )
                once = once + (mat[a][b] * pairs[a, b])
                twice = twice + mat[a][b] * (inner_row + (2.0 * noise_scale) * cross[b][a])
        edge_own[t, 1] = once
        edge_own[t, 2] = twice
        edge_own[t, 3] = sum_own[t]

    for k in range(n_gy):
        edge_send[k] = edge_own[wanted[k]]

    edge_copies = send_all(
        lambda k: edge_send.at[k],
        lambda k: edge_recv.at[k],
        lambda k: edge_send_sem.at[k],
        lambda k: edge_recv_sem.at[k],
    )
    edge_recv[0] = edge_send[0]

    extra_copy.wait()
    for copy in extra_noise_copies:
        copy.wait()
    for wanted_pairs in (early_pairs, late_pairs):

        @pl.loop(0, CHUNKS)
        def _(x):
            lanes = pl.ds(pl.multiple_of(x * LANES, LANES), LANES)
            totals = [jnp.zeros((8, LANES), F32) for _ in wanted_pairs]
            for f in range(EXTRA // HALF):
                fields = pl.ds(f * HALF, HALF)
                parts = [extra[c, fields, lanes] for c in range(3)]
                for s in range(STEPS):
                    parts += [extra_noise[s, c, fields, lanes].astype(F32) for c in range(3)]
                totals = [
                    total + fold(parts[i] * parts[j])
                    for total, (i, j) in zip(totals, wanted_pairs)
                ]
            for pair, total in zip(wanted_pairs, totals):
                extra_second[moment_at[pair], pl.ds(x, 1), :] = row_sum(total)

        if wanted_pairs is early_pairs:
            extra_sum[...] = (
                extra_second[moment_at[0, 0]]
                + extra_second[moment_at[1, 1]]
                + extra_second[moment_at[2, 2]]
            )
            sum_copies = send_all(
                lambda k: extra_sum,
                lambda k: sum_recv.at[k],
                lambda k: sum_send_sem.at[k],
                lambda k: sum_recv_sem.at[k],
            )
            sum_recv[0] = extra_sum[...]

    for copies in (flow_copies, edge_copies):
        for copy in copies:
            copy.wait_recv()
    grads = gradient(
        [flow_recv[my_slot, a] for a in range(3)],
        flow_recv[my_slot, 3],
        flow_recv[my_slot, 4],
        jnp.where(
            block < 3,
            jnp.where(owner > 0, flow_recv[low_slot, 0], 0.0),
            jnp.where(owner < n_gy - 1, flow_recv[high_slot, 0], 0.0),
        ),
        edge_recv[my_slot, 0],
        sub,
        lane,
    )
    first = edge_recv[my_slot, 3]
    rate = relaxation(first + extra_sum[...], 256.0)
    own_share = edge_recv[my_slot, 2] - rate * (2.0 * edge_recv[my_slot, 1] - rate * first)

    def pair_sum(i, j):
        return extra_second[moment_at[min(i, j), max(i, j)]]

    def step_matrix(keep):
        return [
            [grads[3 * a + b] + keep if a == b else grads[3 * a + b] for b in range(3)]
            for a in range(3)
        ]

    def dot(left, right):
        out = left[0] * right[0]
        for u, v in zip(left[1:], right[1:]):
            out = out + u * v
        return out

    one = step_matrix(1.0 - rate)
    total = jnp.zeros((8, LANES), F32)
    for a in range(3):
        mixed = [
            dot(one[a], [pair_sum(i, j) for i in range(3)]) + noise_scale * pair_sum(3 + a, j)
            for j in (0, 1, 2, 3 + a)
        ]
        total = total + dot(one[a], mixed[:3]) + noise_scale * mixed[3]
    moment_recv[0, 6] = total
    two = step_matrix(1.0 - relaxation(total + own_share, 256.0))
    combined = []
    for a in range(3):
        row = [dot(two[a], [one[c][b] for c in range(3)]) for b in range(3)]
        row += [noise_scale * two[a][b] for b in range(3)]
        combined.append(row)
    for a in range(3):
        mixed = [
            dot(combined[a], [pair_sum(i, j) for i in range(6)]) + noise_scale * pair_sum(6 + a, j)
            for j in range(9)
        ]
        for m, (first_axis, second_axis) in enumerate(component_pairs):
            if first_axis == a:
                moment_recv[0, m] = (
                    dot(combined[second_axis], mixed[:6]) + noise_scale * mixed[6 + second_axis]
                )

    moment_copies = send_all(
        lambda k: moment_recv.at[0],
        lambda k: moment_recv.at[k],
        lambda k: moment_send_sem.at[k],
        lambda k: moment_recv_sem.at[k],
    )

    for a in range(3):
        for b in range(6):
            helper_map[6 * a + b] = combined[a][b]

    @pl.loop(0, CHUNKS)
    def _(x):
        lanes = pl.ds(pl.multiple_of(x * LANES, LANES), LANES)
        rows = [
            jnp.broadcast_to(helper_map[n, pl.ds(x, 1), :], (HALF, LANES)) for n in range(18)
        ]
        for f in range(EXTRA // HALF):
            fields = pl.ds(f * HALF, HALF)
            parts = [extra[c, fields, lanes] for c in range(3)]
            parts += [extra_noise[0, c, fields, lanes].astype(F32) for c in range(3)]
            for a in range(3):
                last = extra_noise[1, a, fields, lanes].astype(F32)
                extra[a, fields, lanes] = dot(rows[6 * a : 6 * a + 6], parts) + noise_scale * last

    for copy in sum_copies:
        copy.wait_recv()
    for t in range(TILES):
        slot, hit = slots[t]
        count = jnp.full((CHUNKS, LANES), counts[t], jnp.int32).astype(F32)
        total = sum_own[t] + jnp.where(hit, sum_recv[slot], 0.0)
        rate = relaxation(total, count)
        relax[t] = rate
        own_total[t] = edge_own[t, 2] - rate * (2.0 * edge_own[t, 1] - rate * sum_own[t])

    base_noise_copies[1].wait()

    @pl.loop(0, TILES)
    def _(t):
        for x in range(CHUNKS):
            lanes = pl.ds(x * LANES, LANES)
            mat = matrix(lambda c: tile_grad[t, c, pl.ds(x, 1), :], jnp.ones((1, LANES), F32))
            rate = wide(relax[t, pl.ds(x, 1), :])
            start = [base[t, c, :, lanes] for c in range(3)]
            state = advance(mat, start, [base_noise[t, c, :, lanes] for c in range(3)])
            state = [state[c] - rate * start[c] for c in range(3)]
            for c in range(3):
                base[t, c, :, lanes] = state[c]
            moved = advance(mat, state, [late_noise[t, c, :, lanes] for c in range(3)])
            for c in range(3):
                drifted[t, c, :, lanes] = moved[c]
            for m, (a, b) in enumerate(component_pairs):
                here = pl.ds(x, 1)
                own_rows[t, m, here, :] = row_sum(fold(moved[a] * moved[b]))
                if a == b:
                    own_rows[t, 6 + m, here, :] = 2.0 * row_sum(fold(moved[a] * state[a]))
                else:
                    both = fold(moved[a] * state[b] + moved[b] * state[a])
                    own_rows[t, 6 + m, here, :] = row_sum(both)
                own_rows[t, 12 + m, here, :] = row_sum(fold(state[a] * state[b]))

    for copies in (halo_copies, flow_copies, sum_copies, edge_copies):
        for copy in copies:
            copy.wait_send()
    for copy in moment_copies:
        copy.wait_recv()
        copy.wait_send()


def finish_kernel(
    n_gy,
    counts_hbm,
    helper_hbm,
    start,
    drifted,
    extra,
    own_total,
    own_rows,
    moment_recv,
    base_out,
    extra_out,
    stress_out,
    counts,
    helper,
    base,
    stress,
    staged,
    relax,
    tile_sem,
    out_sem,
):
    gy = lax.axis_index("gy")
    helper_copy = pltpu.make_async_copy(helper_hbm, helper, out_sem.at[2])
    counts_copy = pltpu.make_async_copy(counts_hbm, counts, out_sem.at[3])
    extra_copy = pltpu.make_async_copy(extra, extra_out, out_sem.at[0])
    helper_copy.start()
    counts_copy.start()
    extra_copy.start()
    helper_copy.wait()
    counts_copy.wait()
    slots = helper_slots(helper, gy, n_gy)
    tile_counts = [jnp.full((CHUNKS, LANES), counts[t], jnp.int32).astype(F32) for t in range(TILES)]
    for t in range(TILES):
        slot, hit = slots[t]
        total = own_total[t] + jnp.where(hit, moment_recv[slot, 6], 0.0)
        relax[t] = relaxation(total, tile_counts[t])

    @pl.loop(0, TILES)
    def _(t):
        for x in range(CHUNKS):
            lanes = pl.ds(x * LANES, LANES)
            rate = wide(relax[t, pl.ds(x, 1), :])
            for c in range(3):
                base[t, c, :, lanes] = drifted[t, c, :, lanes] - rate * start[t, c, :, lanes]
        pltpu.make_async_copy(base.at[t], base_out.at[t], tile_sem.at[t]).start()

    for t in range(TILES):
        slot, hit = slots[t]
        rate = relax[t]
        second = []
        for m in range(6):
            own = own_rows[t, m] - rate * (own_rows[t, 6 + m] - rate * own_rows[t, 12 + m])
            second.append((own + jnp.where(hit, moment_recv[slot, m], 0.0)) / tile_counts[t])
        trace = second[0] + second[1] + second[2]
        stretch = 1.0 / (1.0 - trace / max_extension)
        for m in range(6):
            staged[m, :, t, :] = (stretch * second[m] - (1.0 if m < 3 else 0.0)) / weissenberg

    for m in range(6):
        for x in range(CHUNKS):
            stress[m, :, pl.ds(x * LANES, LANES)] = staged[m, x]

    stress_copy = pltpu.make_async_copy(stress, stress_out, out_sem.at[1])
    stress_copy.start()
    for t in range(TILES):
        pltpu.make_async_copy(base.at[t], base_out.at[t], tile_sem.at[t]).wait()
    extra_copy.wait()
    stress_copy.wait()


def hold(array):
    return pltpu.with_memory_space_constraint(array, pltpu.HBM)


def solution(mesh):
    n_gx, n_gy = mesh.shape["gx"], mesh.shape["gy"]

    def per_device(
        velocity,
        wall_cells,
        tile_counts,
        helper_tile,
        base_fields,
        extra_fields,
        base_noise,
        extra_noise,
    ):
        hbm = pl.BlockSpec(memory_space=pltpu.HBM)
        vmem = pl.BlockSpec(memory_space=pltpu.VMEM)
        dma = pltpu.SemaphoreType.DMA
        counts = hold(tile_counts.reshape(TILES))
        helper = hold(helper_tile.reshape(n_gy))

        def block(*lead):
            return pltpu.VMEM((*lead, CHUNKS, LANES), F32)

        passed = pl.pallas_call(
            functools.partial(exchange_kernel, n_gx, n_gy),
            out_shape=(
                jax.ShapeDtypeStruct((TILES, 3, BASE, CELLS), F32),
                jax.ShapeDtypeStruct((TILES, 3, BASE, CELLS), F32),
                jax.ShapeDtypeStruct((3, EXTRA, CELLS), F32),
                jax.ShapeDtypeStruct((TILES, CHUNKS, LANES), F32),
                jax.ShapeDtypeStruct((TILES, 18, CHUNKS, LANES), F32),
                jax.ShapeDtypeStruct((n_gy, 7, CHUNKS, LANES), F32),
            ),
            in_specs=[hbm] * 8,
            out_specs=(vmem,) * 6,
            scratch_shapes=[
                pltpu.SMEM((TILES,), jnp.int32),
                pltpu.SMEM((n_gy,), jnp.int32),
                block(3, 8),
                pltpu.VMEM((8, 8, LANES), jnp.int32),
                pltpu.VMEM((TILES, 3, BASE, CELLS), jnp.bfloat16),
                pltpu.VMEM((TILES, 3, BASE, CELLS), jnp.bfloat16),
                pltpu.VMEM((STEPS, 3, EXTRA, CELLS), jnp.bfloat16),
                block(2, 3),
                block(8),
                block(6),
                block(TILES, 16),
                block(TILES),
                block(TILES, 5),
                block(n_gy, 5),
                block(n_gy, 5),
                block(TILES),
                block(),
                block(n_gy),
                block(TILES, 4),
                block(n_gy, 4),
                block(n_gy, 4),
                block(45),
                block(18),
                block(TILES, 9),
                block(TILES),
                dma((9,)),
                dma((TILES,)),
                dma((4,)),
                dma((4,)),
                dma((n_gy,)),
                dma((n_gy,)),
                dma((n_gy,)),
                dma((n_gy,)),
                dma((n_gy,)),
                dma((n_gy,)),
                dma((n_gy,)),
                dma((n_gy,)),
                pltpu.SemaphoreType.REGULAR,
            ],
            compiler_params=pltpu.CompilerParams(
                collective_id=0, has_side_effects=True, vmem_limit_bytes=40 << 20
            ),
        )(
            counts,
            helper,
            hold(velocity),
            hold(wall_cells),
            hold(base_fields.reshape(TILES, 3, BASE, CELLS)),
            hold(extra_fields.reshape(3, EXTRA, CELLS)),
            hold(base_noise.reshape(TILES, STEPS, 3, BASE, CELLS)),
            hold(extra_noise.reshape(STEPS, 3, EXTRA, CELLS)),
        )
        base_out, extra_out, stress_out = pl.pallas_call(
            functools.partial(finish_kernel, n_gy),
            out_shape=(
                jax.ShapeDtypeStruct((TILES, 3, BASE, CELLS), F32),
                jax.ShapeDtypeStruct((3, EXTRA, CELLS), F32),
                jax.ShapeDtypeStruct((6, TILES, CELLS), F32),
            ),
            in_specs=[hbm] * 2 + [vmem] * 6,
            out_specs=(hbm,) * 3,
            scratch_shapes=[
                pltpu.SMEM((TILES,), jnp.int32),
                pltpu.SMEM((n_gy,), jnp.int32),
                pltpu.VMEM((TILES, 3, BASE, CELLS), F32),
                pltpu.VMEM((6, TILES, CELLS), F32),
                pltpu.VMEM((6, CHUNKS, TILES, LANES), F32),
                block(TILES),
                dma((TILES,)),
                dma((4,)),
            ],
            compiler_params=pltpu.CompilerParams(vmem_limit_bytes=40 << 20),
        )(counts, helper, *passed)
        return base_out[None, None], extra_out[None, None], stress_out.transpose(1, 0, 2)[None, None]

    in_specs = (
        P(None, "gx", "gy", None),
        P("gx", "gy", None),
        P("gx", "gy", None),
        P("gx", None),
        P("gx", "gy", None, None, None, None),
        P("gx", "gy", None, None, None),
        P("gx", "gy", None, None, None, None, None),
        P("gx", "gy", None, None, None, None),
    )
    out_specs = (
        P("gx", "gy", None, None, None, None),
        P("gx", "gy", None, None, None),
        P("gx", "gy", None, None, None),
    )
    return jax.shard_map(
        per_device, mesh=mesh, in_specs=in_specs, out_specs=out_specs, check_vma=False
    )
```
